128 devices in a mesh: row: 8 (over z, y_hi), col: 16 (over y_lo, x, core).
Axes of the slice: x: 4, y: 4 (y_hi: 2, y_lo: 2; y = y_hi * 2 + y_lo), z: 4, core: 2. Of those that a mesh axis runs over, the one named last changes fastest.
Arguments:
- v_coef: float32 [2, 512, 768, 256], P(None, 'col', 'row'), may hold values from -0.75 to 0.75
- vort_coef: float32 [2, 512, 768, 256], P(None, 'col', 'row'), may hold values from -6 to 6
- plane_ops: float32 [3, 24, 256], replicated, may hold values from -0.375 to 0.375
- inverse_ops: float32 [2, 256, 24], replicated, may hold values from -1.25 to 1.25
Outputs:
- vort_rhs: float32 [2, 512, 768, 256], P(None, 'col', 'row')
- lapv_rhs: float32 [2, 512, 768, 256], P(None, 'col', 'row')
The draws below stay inside these ranges and needn't reach their ends.
All inputs are finite; a program needn't handle non-finite values.
Results may differ from the reference program's by a relative error of at most 0.00012.
Values sent between devices are 32-bit elements; how exact they have to be, the bound alone decides.
No kernel may reach another device: no remote copies, remote signals or barrier semaphores. Data moves between devices by JAX's collectives and lax.ppermute only.
A program may use at most 192 MiB of HBM per device.

```python
import jax
import jax.numpy as jnp
from jax import lax

KX = 512
KZ = 768
NY = 256
PLANES = 24


def spectrum(key, amplitude):
    stream_modes = jnp.arange(KX, dtype=jnp.int32).astype(jnp.float32) * 0.25
    span_index = jnp.arange(KZ, dtype=jnp.int32)
    signed = jnp.where(span_index < KZ // 2, span_index, span_index - KZ).astype(jnp.float32) * (2.0 / 3.0)
    square = stream_modes[:, None] * stream_modes[:, None] + signed[None, :] * signed[None, :]
    shaping = amplitude / (1.0 + square / 256.0)
    gaussian = jax.random.truncated_normal(key, -6.0, 6.0, (2, KX, KZ, NY), jnp.float32)
    return gaussian * shaping[None, :, :, None]


def draw_v_coef(key, part):
    return spectrum(jax.random.fold_in(key, 3), 0.125)


def draw_vort_coef(key, part):
    return spectrum(jax.random.fold_in(key, 7), 1.0)


def bell_draw(rng, extent, spread, reach, kind=jnp.bfloat16):
    return jnp.clip(spread * jax.random.normal(rng, extent, jnp.float32), -reach, reach).astype(kind)


def setup_inputs(seed: int = 0) -> dict:
    arg_keys = jax.random.split(jax.random.key(seed), 5)
    return {
        "v_coef": draw_v_coef(jax.random.fold_in(arg_keys[4], 71), 0),
        "vort_coef": draw_vort_coef(jax.random.fold_in(arg_keys[4], 71), 0),
        "plane_ops": bell_draw(arg_keys[2], (3, PLANES, NY), NY ** -0.5, 0.375, jnp.float32),
        "inverse_ops": bell_draw(arg_keys[3], (2, NY, PLANES), PLANES ** -0.5, 1.25, jnp.float32),
    }


PRECISE = lax.Precision.HIGHEST
STREAM_STEP = 0.25
SPAN_STEP = 2.0 / 3.0
INVERSE_SCALE = 1.0 / 32.0
FORWARD_SCALE = 32.0

def reference(v_coef, vort_coef, plane_ops, inverse_ops):
    points_x = 3 * KX
    points_z = 3 * KZ // 2
    half = KZ // 2
    stream = (STREAM_STEP * jnp.arange(KX, dtype=jnp.int32).astype(jnp.float32))[:, None]
    span_index = jnp.arange(KZ, dtype=jnp.int32)
    signed = jnp.where(span_index < half, span_index, span_index - KZ)
    span = (SPAN_STEP * signed.astype(jnp.float32))[None, :]
    square = stream * stream + span * span
    recip = 1.0 / jnp.where(square > 0, square, 1.0)
    v_values = jnp.einsum('rpj,cxkj->rpcxk', plane_ops, v_coef, precision=PRECISE)
    g_values = jnp.einsum('rpj,cxkj->rpcxk', plane_ops[:2], vort_coef, precision=PRECISE)
    v_cplx = v_values[:, :, 0] + 1j * v_values[:, :, 1]
    g_cplx = g_values[:, :, 0] + 1j * g_values[:, :, 1]
    v_base, v_slope, v_curve = (v_cplx[0], v_cplx[1], v_cplx[2])
    g_base, g_slope = (g_cplx[0], g_cplx[1])
    along = (1j * stream * v_slope - 1j * span * g_base) * recip
    across = (1j * span * v_slope + 1j * stream * g_base) * recip
    omega_x = (1j * span * v_curve + 1j * stream * g_slope) * recip - 1j * span * v_base
    omega_z = 1j * stream * v_base - (1j * stream * v_curve - 1j * span * g_slope) * recip
    fields = jnp.stack([along, v_base, across, omega_x, g_base, omega_z], axis=1)

    def one_plane(slab):
        padded = jnp.zeros((6, KX, points_z), slab.dtype)
        padded = padded.at[:, :, :half].set(slab[:, :, :half])
        padded = padded.at[:, :, points_z - half:].set(slab[:, :, half:])
        span_phys = jnp.fft.ifft(padded, axis=-1) * points_z
        wide = jnp.zeros((6, points_x // 2 + 1, points_z), slab.dtype)
        wide = wide.at[:, :KX].set(span_phys)
        physical_space = jnp.fft.irfft(wide, n=points_x, axis=1) * (points_x * INVERSE_SCALE)
        velocity_field = physical_space[0:3]
        vorticity_field = physical_space[3:6]
        product_streamwise = velocity_field[1] * vorticity_field[2] - velocity_field[2] * vorticity_field[1]
        product_normal = velocity_field[2] * vorticity_field[0] - velocity_field[0] * vorticity_field[2]
        product_spanwise = velocity_field[0] * vorticity_field[1] - velocity_field[1] * vorticity_field[0]
        products = jnp.stack([product_streamwise, product_normal, product_spanwise], axis=0)
        stream_spec = jnp.fft.rfft(products, axis=1)[:, :KX] / points_x
        full_spec = jnp.fft.fft(stream_spec, axis=-1) * (FORWARD_SCALE / points_z)
        return jnp.concatenate([full_spec[:, :, :half], full_spec[:, :, points_z - half:]], axis=-1)
    spectral = lax.map(one_plane, fields)
    h_x, h_y, h_z = (spectral[:, 0], spectral[:, 1], spectral[:, 2])
    g_term = 1j * span * h_x - 1j * stream * h_z
    s_term = -(1j * stream * h_x + 1j * span * h_z)
    y_term = -square * h_y
    damp_g = 1.0 / jnp.sqrt(1.0 + square)
    damp_v = 1.0 / (1.0 + square)

    def contract(matrix, term):
        real_part = jnp.einsum('jp,pxk->xkj', matrix, jnp.real(term), precision=PRECISE)
        imag_part = jnp.einsum('jp,pxk->xkj', matrix, jnp.imag(term), precision=PRECISE)
        return jnp.stack([real_part, imag_part], axis=0)
    vort_rhs = contract(inverse_ops[0], g_term) * damp_g[None, :, :, None]
    lapv_sum = contract(inverse_ops[1], s_term) + contract(inverse_ops[0], y_term)
    lapv_rhs = lapv_sum * damp_v[None, :, :, None]
    return (vort_rhs, lapv_rhs)
```

```python
import math

import jax
import jax.numpy as jnp
import ml_dtypes
import numpy as np
from jax import lax
from jax.experimental import pallas as pl
from jax.experimental.pallas import tpu as pltpu
from jax.sharding import PartitionSpec as P

STREAM_STEP = 0.25
SPAN_STEP = 2.0 / 3.0
ROWS = 8
COLS = 16
KX = 512
KZ = 768
NY = 256
PLANES = 24
CHUNKS = PLANES // ROWS
XL = KX // COLS
KL = KZ // ROWS
POINTS_X = 3 * KX
POINTS_Z = 3 * KZ // 2
HALF_X = POINTS_X // 2
HALF_Z = POINTS_Z // 2
ZL = POINTS_Z // COLS
GROUPS = XL // 4
SLOTS = KL // 32
PART = SLOTS * GROUPS
F32 = jnp.float32
BF16 = jnp.bfloat16
VMEM_LIMIT = 56 * 1024 * 1024


def parts(table):
    table = np.asarray(table, np.float64)
    high = table.astype(np.float32).astype(ml_dtypes.bfloat16)
    low = (table - high.astype(np.float64)).astype(np.float32).astype(ml_dtypes.bfloat16)
    return [high, low]


def span_order():
    lane = np.arange(KZ)
    slot, rest = lane // (32 * ROWS), lane % (32 * ROWS)
    return (rest // 32) * KL + slot * 32 + rest % 32


def span_signed(modes):
    return np.where(modes < KZ // 2, modes, modes - KZ)


def stream_order():
    index = np.arange(KX)
    col, rest = index // XL, index % XL
    return col * XL + 4 * (rest % GROUPS) + rest // GROUPS


def span_angle(points):
    signed = span_signed(span_order())
    turn = np.mod((2 * points[:, None] + 1) * signed[None, :], 2 * POINTS_Z)
    return turn * (math.pi / POINTS_Z)


def span_inverse_tables():
    angle = span_angle(np.arange(HALF_Z))
    return parts(np.cos(angle)) + parts(np.sin(angle))


def span_forward_tables():
    main = (np.arange(8)[:, None] * ZL + np.arange(64)[None, :]).reshape(-1)
    tail = np.arange(8)[:, None, None] * ZL + 64 + np.arange(8)[None, None, :]
    tail = np.broadcast_to(tail, (8, 3, 8)).reshape(-1)
    points = np.concatenate([main, tail, np.zeros(64, np.int64)])
    used = (np.arange(points.size) < 704)[:, None]
    factor = used * (32.0 / POINTS_Z)
    angle = span_angle(points)
    return parts(np.cos(angle) * factor) + parts(np.sin(angle) * factor)


def stream_angle():
    turn = np.mod(stream_order()[:, None] * (2 * np.arange(HALF_X)[None, :] + 1), 2 * POINTS_X)
    return turn * (math.pi / POINTS_X)


def stream_inverse_tables():
    weight = np.where(stream_order() == 0, 1.0, 2.0)[:, None] / 32.0
    angle = stream_angle()
    return parts(weight * np.cos(angle)) + parts(-weight * np.sin(angle))


def stream_forward_tables():
    angle = stream_angle()
    return parts(np.cos(angle) / POINTS_X) + parts(-np.sin(angle) / POINTS_X)


def span_lanes():
    signed = span_signed(span_order())
    half = signed * (math.pi / POINTS_Z)
    rows = np.zeros((8, KZ), np.float32)
    rows[0] = np.cos(half)
    rows[1] = np.sin(half)
    return rows


def split(value):
    high = value.astype(BF16)
    low = (value - high.astype(F32)).astype(BF16)
    return high, low


def dot_nn(left, right):
    return lax.dot_general(left, right, (((1,), (0,)), ((), ())), preferred_element_type=F32)


def dot_nt(left, right):
    return lax.dot_general(left, right, (((1,), (1,)), ((), ())), preferred_element_type=F32)


def dot_tn(left, right):
    return lax.dot_general(left, right, (((0,), (0,)), ((), ())), preferred_element_type=F32)


def triple(dot, left, right):
    return dot(left[0], right[0]) + (dot(left[0], right[1]) + dot(left[1], right[0]))


def swap_blocks(tiles):
    lane = lax.broadcasted_iota(jnp.int32, tiles[0].shape, 1)
    low64 = lane < 64
    low32 = (lane & 32) == 0

    def turn(value, amount):
        return pltpu.roll(value, amount, 1)

    a0 = jnp.where(low64, tiles[0], turn(tiles[2], 64))
    a2 = jnp.where(low64, turn(tiles[0], 64), tiles[2])
    a1 = jnp.where(low64, tiles[1], turn(tiles[3], 64))
    a3 = jnp.where(low64, turn(tiles[1], 64), tiles[3])
    b0 = jnp.where(low32, a0, turn(a1, 32))
    b1 = jnp.where(low32, turn(a0, 96), a1)
    b2 = jnp.where(low32, a2, turn(a3, 32))
    b3 = jnp.where(low32, turn(a2, 96), a3)
    return [b0, b1, b2, b3]


def whole(shape):
    zeros = (0,) * len(shape)
    return pl.BlockSpec(shape, lambda *_: zeros)


def params(axes=1):
    return pltpu.CompilerParams(
        dimension_semantics=("arbitrary",) * axes, vmem_limit_bytes=VMEM_LIMIT
    )


PLANE_ROWS = 5 * 2 * PART


def plane_kernel(ops_ref, v_ref, g_ref, *out_refs):
    group = pl.program_id(0)
    ops = split(ops_ref[...])

    def gathered(ref):
        pieces = []
        for c in range(2):
            for slot in range(SLOTS):
                for t in range(4):
                    pieces.append(ref[c, t, 32 * slot : 32 * slot + 32, :])
        return split(jnp.concatenate(pieces, axis=0))

    v_values = triple(dot_nt, ops, gathered(v_ref))
    g_values = triple(dot_nt, [part[: 2 * PLANES] for part in ops], gathered(g_ref))
    for value in range(5):
        source = v_values if value < 3 else g_values
        first = (value if value < 3 else value - 3) * PLANES
        for chunk in range(CHUNKS):
            top = first + chunk * ROWS
            for c in range(2):
                for slot in range(SLOTS):
                    lane = (c * SLOTS + slot) * 128
                    row = (value * 2 + c) * PART + slot * GROUPS + group
                    out_refs[chunk][pl.ds(row, ROWS, stride=PLANE_ROWS), :] = source[
                        top : top + ROWS, lane : lane + 128
                    ]


def plane_values(plane_ops, v_coef, vort_coef):
    out = jax.ShapeDtypeStruct((ROWS * PLANE_ROWS, 128), F32)
    coef = pl.BlockSpec((2, 4, KL, NY), lambda q: (0, q, 0, 0))
    return pl.pallas_call(
        plane_kernel,
        grid=(GROUPS,),
        in_specs=[whole((3 * PLANES, NY)), coef, coef],
        out_specs=[whole(out.shape)] * CHUNKS,
        out_shape=[out] * CHUNKS,
        compiler_params=params(),
        name="plane_values",
    )(plane_ops.reshape(3 * PLANES, NY), v_coef, vort_coef)


def span_inverse_kernel(in_ref, wave_ref, lanes_ref, ch, cl, sh, sl, out_ref, dh, dl, eh, el):
    blocks = []
    for quad in range(ROWS // 4):
        blocks.append(swap_blocks([in_ref[4 * quad + i] for i in range(4)]))

    def value(index, c):
        top = (index * 2 + c) * PART
        rows = []
        for t in range(4):
            lanes = []
            for slot in range(SLOTS):
                at = top + slot * GROUPS
                for quad in range(ROWS // 4):
                    lanes.append(blocks[quad][t][at : at + GROUPS])
            rows.append(jnp.concatenate(lanes, axis=1))
        return jnp.concatenate(rows, axis=0)

    cosine = lanes_ref[0:1, :]
    sine = lanes_ref[1:2, :]

    def turned(index):
        re, im = value(index, 0), value(index, 1)
        return (re * cosine + im * sine, im * cosine - re * sine)

    v_base, v_slope, v_curve, g_base, g_slope = [turned(i) for i in range(5)]
    along, across = wave_ref[0], wave_ref[1]
    stream, span = wave_ref[2], wave_ref[3]

    def times_i(pair):
        return (-pair[1], pair[0])

    fields = [
        times_i([along * v_slope[c] - across * g_base[c] for c in range(2)]),
        v_base,
        times_i([across * v_slope[c] + along * g_base[c] for c in range(2)]),
        times_i(
            [across * v_curve[c] + along * g_slope[c] - span * v_base[c] for c in range(2)]
        ),
        g_base,
        times_i(
            [stream * v_base[c] - along * v_curve[c] + across * g_slope[c] for c in range(2)]
        ),
    ]
    for f, pair in enumerate(fields):
        top = f * 2 * XL
        re_high, re_low = split(pair[0])
        im_high, im_low = split(pair[1])
        dh[top : top + XL, :] = re_high
        dl[top : top + XL, :] = re_low
        dh[top + XL : top + 2 * XL, :] = im_high
        dl[top + XL : top + 2 * XL, :] = im_low
        eh[top : top + XL, :] = -im_high
        el[top : top + XL, :] = -im_low
        eh[top + XL : top + 2 * XL, :] = re_high
        el[top + XL : top + 2 * XL, :] = re_low
    straight = [dh[...], dl[...]]
    crossed = [eh[...], el[...]]
    for pair in range(COLS // 4):
        rows = slice(pair * 2 * ZL, (pair + 1) * 2 * ZL)
        even = triple(dot_nt, [ch[rows, :], cl[rows, :]], straight)
        odd = triple(dot_nt, [sh[rows, :], sl[rows, :]], crossed)
        plus, minus = even + odd, even - odd
        for half in range(2):
            part = slice(half * ZL, (half + 1) * ZL)
            out_ref[4 * pair + 2 * half] = plus[part]
            out_ref[4 * pair + 2 * half + 1] = minus[part]


def span_inverse(received, wave, lanes, tables):
    out = jax.ShapeDtypeStruct((COLS, ZL, 12 * XL), F32)
    args = [received, wave, lanes] + tables
    return pl.pallas_call(
        span_inverse_kernel,
        grid=(1,),
        in_specs=[whole(a.shape) for a in args],
        out_specs=whole(out.shape),
        out_shape=out,
        scratch_shapes=[pltpu.VMEM((12 * XL, KZ), BF16)] * 4,
        compiler_params=params(),
        name="span_inverse",
    )(*args)


BLOCK_X = 256


def product_kernel(in_ref, ch, cl, sh, sl, fch, fcl, fsh, fsl, out_ref, modes):
    for quad in range(COLS // 4):
        for column in range(3):
            tiles = [in_ref[4 * quad + i, :, column * 128 : column * 128 + 128] for i in range(4)]
            for slot, tile in enumerate(swap_blocks(tiles)):
                top = (2 * column + slot // 2) * ZL
                modes[slot % 2, top : top + ZL, quad * 128 : quad * 128 + 128] = tile
    real = split(modes[0])
    imag = split(modes[1])
    total_re, total_im = None, None
    for block in range(HALF_X // BLOCK_X):
        here = slice(block * BLOCK_X, (block + 1) * BLOCK_X)
        even = triple(dot_nn, real, [ch[:, here], cl[:, here]])
        odd = triple(dot_nn, imag, [sh[:, here], sl[:, here]])

        def products(field):
            u, v, w, ox, oy, oz = [field[i * ZL : (i + 1) * ZL] for i in range(6)]
            return [v * oz - w * oy, w * ox - u * oz, u * oy - v * ox]

        right = products(even + odd)
        left = products(even - odd)

        def ordered(values):
            zeros = jnp.zeros((256 - 3 * ZL, BLOCK_X), F32)
            pieces = [x[:64] for x in values] + [x[64:] for x in values] + [zeros]
            return split(jnp.concatenate(pieces, axis=0))

        sums = ordered([r + l for r, l in zip(right, left)])
        gaps = ordered([r - l for r, l in zip(right, left)])
        part_re = triple(dot_nt, [fch[:, here], fcl[:, here]], sums)
        part_im = triple(dot_nt, [fsh[:, here], fsl[:, here]], gaps)
        total_re = part_re if total_re is None else total_re + part_re
        total_im = part_im if total_im is None else total_im + part_im
    for col in range(COLS):
        rows = slice(col * XL, (col + 1) * XL)
        out_ref[col, 0] = total_re[rows]
        out_ref[col, 1] = total_im[rows]


def stream_products(received, tables):
    out = jax.ShapeDtypeStruct((COLS, 2, XL, 256), F32)
    args = [received] + tables
    return pl.pallas_call(
        product_kernel,
        grid=(1,),
        in_specs=[whole(a.shape) for a in args],
        out_specs=whole(out.shape),
        out_shape=out,
        scratch_shapes=[pltpu.VMEM((2, 6 * ZL, KX), F32)],
        compiler_params=params(),
        name="stream_products",
    )(*args)


HOME_ROWS = 2 * 3 * PART


def span_forward_kernel(in_ref, lanes_ref, ch, cl, sh, sl, out_ref):
    sums, gaps = [], []
    for pair in range(8):
        plus = in_ref[2 * pair].reshape(2 * XL, 256)
        minus = in_ref[2 * pair + 1].reshape(2 * XL, 256)
        sums.append(plus + minus)
        gaps.append(plus - minus)
    lane = lax.broadcasted_iota(jnp.int32, (2 * XL, 128), 1)
    low64 = lane < 64

    def ordered(values):
        firsts = [x[:, :128] for x in values]
        lasts = [x[:, 128:] for x in values]
        main = [[], [], []]
        for i in range(0, 8, 2):
            a, b = firsts[i], firsts[i + 1]
            main[0].append(jnp.where(low64, a, pltpu.roll(b, 64, 1)))
            main[1].append(jnp.where(low64, pltpu.roll(a, 64, 1), b))
            main[2].append(jnp.where(low64, lasts[i], pltpu.roll(lasts[i + 1], 64, 1)))
        tails = [jnp.zeros_like(lasts[0]), jnp.zeros_like(lasts[0])]
        for i in range(8):
            start = 24 * i
            for half in range(2):
                low, high = max(start, 128 * half), min(start + 24, 128 * half + 128)
                if low >= high:
                    continue
                shift = (start - 64) % 128
                moved = pltpu.roll(lasts[i], shift, 1) if shift else lasts[i]
                inside = (lane >= low - 128 * half) & (lane < high - 128 * half)
                tails[half] = jnp.where(inside, moved, tails[half])
        out = []
        for h in range(3):
            ends = []
            for half in range(2):
                index = lane + 128 * half
                mine = ((index // 8) % 3 == h) & (index < 192)
                ends.append(jnp.where(mine, tails[half], 0.0))
            out.append(jnp.concatenate(main[h] + ends, axis=1))
        return out

    e_rows, o_rows = [], []
    even, odd = ordered(sums), ordered(gaps)
    for c in range(2):
        for h in range(3):
            e_rows.append(even[h][c * XL : (c + 1) * XL])
            o_rows.append(odd[h][XL:] if c == 0 else -odd[h][:XL])
    left = split(jnp.concatenate(e_rows, axis=0))
    right = split(jnp.concatenate(o_rows, axis=0))
    result = triple(dot_nn, left, [ch[...], cl[...]]) + triple(dot_nn, right, [sh[...], sl[...]])
    cosine = lanes_ref[0:1, :]
    sine = lanes_ref[1:2, :]
    re, im = result[: 3 * XL], result[3 * XL :]
    turned = [re * cosine - im * sine, re * sine + im * cosine]
    for c in range(2):
        for h in range(3):
            block = turned[c][h * XL : (h + 1) * XL]
            for slot in range(SLOTS):
                top = (c * 3 + h) * PART + slot * GROUPS
                for quad in range(ROWS // 4):
                    at = slot * 256 + quad * 128
                    tiles = [block[t * 8 : t * 8 + 8, at : at + 128] for t in range(4)]
                    for i, tile in enumerate(swap_blocks(tiles)):
                        out_ref[4 * quad + i, top : top + GROUPS, :] = tile


def span_forward(received, lanes, tables):
    out = jax.ShapeDtypeStruct((ROWS, HOME_ROWS, 128), F32)
    args = [received, lanes] + tables
    return pl.pallas_call(
        span_forward_kernel,
        grid=(1,),
        in_specs=[whole(a.shape) for a in args],
        out_specs=whole(out.shape),
        out_shape=out,
        compiler_params=params(),
        name="span_forward",
    )(*args)


def combine_kernel(*refs):
    in_refs, (factor_ref, inverse_ref, vort_ref, lapv_ref) = refs[:CHUNKS], refs[CHUNKS:]
    group = pl.program_id(0)

    def stacked(value):
        high = value.astype(BF16).astype(F32)
        return high, value - high

    g_lanes, s_lanes = [], []
    for slot in range(SLOTS):
        factors = [factor_ref[i, pl.ds(slot * GROUPS + group, 1), :] for i in range(5)]

        def field(h, c):
            row = (c * 3 + h) * PART + slot * GROUPS + group
            return jnp.concatenate(
                [ref[pl.ds(row, ROWS, stride=HOME_ROWS), :] for ref in in_refs], axis=0
            )

        hx = [field(0, c) for c in range(2)]
        hy = [field(1, c) for c in range(2)]
        hz = [field(2, c) for c in range(2)]
        for c in range(2):
            other = 1 - c
            g_term = factors[0] * hx[other] - factors[1] * hz[other]
            s_term = factors[2] * hx[other] + factors[3] * hz[other]
            if c == 0:
                g_term = -g_term
            else:
                s_term = -s_term
            y_term = factors[4] * hy[c]
            gh, gl = stacked(g_term)
            sh, sl = stacked(s_term)
            yh, yl = stacked(y_term)
            g_lanes.append(jnp.concatenate([gh, gl, gh], axis=0))
            s_lanes.append(jnp.concatenate([sh, sl, sh, yh, yl, yh], axis=0))
    g_left = jnp.concatenate(g_lanes, axis=1).astype(BF16)
    s_left = jnp.concatenate(s_lanes, axis=1).astype(BF16)

    def right(index):
        high, low = stacked(inverse_ref[index])
        return jnp.concatenate([high, high, low], axis=0)

    first, second = right(0), right(1)
    vort = dot_tn(g_left, first.astype(BF16))
    lapv = dot_tn(s_left, jnp.concatenate([second, first], axis=0).astype(BF16))
    for slot in range(SLOTS):
        for c in range(2):
            for t in range(4):
                row = (slot * 2 + c) * 128 + t * 32
                vort_ref[c, t, 32 * slot : 32 * slot + 32, :] = vort[row : row + 32]
                lapv_ref[c, t, 32 * slot : 32 * slot + 32, :] = lapv[row : row + 32]


def combine_planes(received, factors, inverse_ops):
    out = jax.ShapeDtypeStruct((2, XL, KL, NY), F32)
    args = list(received) + [factors, jnp.swapaxes(inverse_ops, 1, 2)]
    block = pl.BlockSpec((2, 4, KL, NY), lambda q: (0, q, 0, 0))
    return pl.pallas_call(
        combine_kernel,
        grid=(GROUPS,),
        in_specs=[whole(a.shape) for a in args],
        out_specs=[block, block],
        out_shape=[out, out],
        compiler_params=params(),
        name="combine_planes",
    )(*args)


def span_wave_arrays():
    row = jnp.arange(XL, dtype=jnp.int32)
    x = 4 * (row % GROUPS) + row // GROUPS + lax.axis_index("col") * XL
    stream = (STREAM_STEP * x.astype(F32))[:, None]
    signed = jnp.asarray(span_signed(span_order()), jnp.int32)
    span = (SPAN_STEP * signed.astype(F32))[None, :]
    square = stream * stream + span * span
    recip = 1.0 / jnp.where(square > 0, square, 1.0)
    full = jnp.zeros_like(square)
    return jnp.stack([stream * recip, span * recip, stream + full, span + full], axis=0)


def home_factors():
    part = jnp.arange(PART, dtype=jnp.int32)[:, None]
    lane = jnp.arange(128, dtype=jnp.int32)[None, :]
    x = 4 * (part % GROUPS) + lane // 32 + lax.axis_index("col") * XL
    k = 32 * (part // GROUPS) + lane % 32 + lax.axis_index("row") * KL
    stream = STREAM_STEP * x.astype(F32)
    span = SPAN_STEP * jnp.where(k < KZ // 2, k, k - KZ).astype(F32)
    square = stream * stream + span * span
    damp_g = 1.0 / jnp.sqrt(1.0 + square)
    damp_v = 1.0 / (1.0 + square)
    return jnp.stack(
        [damp_g * span, damp_g * stream, damp_v * stream, damp_v * span, -damp_v * square], axis=0
    )


def exchange(value, axis):
    return lax.all_to_all(value, axis, split_axis=0, concat_axis=0, tiled=True)


def per_device(v_coef, vort_coef, plane_ops, inverse_ops):
    def constants(arrays):
        return [jnp.asarray(a) for a in arrays]

    span_in = constants(span_inverse_tables())
    span_out = constants(span_forward_tables())
    stream = constants(stream_inverse_tables() + stream_forward_tables())
    lanes = jnp.asarray(span_lanes())
    wave = span_wave_arrays()
    factors = home_factors()
    values = plane_values(plane_ops, v_coef, vort_coef)
    home = []
    for value in values:
        pencils = exchange(value.reshape(ROWS, PLANE_ROWS, 128), "row")
        sent = span_inverse(pencils, wave, lanes, span_in)
        arrived = exchange(sent, "col")
        returned = exchange(stream_products(arrived, stream), "col")
        full = exchange(span_forward(returned, lanes, span_out), "row")
        home.append(full.reshape(ROWS * HOME_ROWS, 128))
    vort_rhs, lapv_rhs = combine_planes(home, factors, inverse_ops)
    return (vort_rhs, lapv_rhs)


def solution(mesh):
    in_specs = (P(None, "col", "row", None), P(None, "col", "row", None), P(), P())
    out_specs = (P(None, "col", "row", None), P(None, "col", "row", None))
    return jax.shard_map(
        per_device, mesh=mesh, in_specs=in_specs, out_specs=out_specs, check_vma=False
    )
```

```python
import math

import jax
import jax.numpy as jnp
import ml_dtypes
import numpy as np
from jax import lax
from jax.experimental import pallas as pl
from jax.experimental.pallas import tpu as pltpu
from jax.sharding import PartitionSpec as P

STREAM_STEP = 0.25
SPAN_STEP = 2.0 / 3.0
ROWS = 8
COLS = 16
KX = 512
KZ = 768
NY = 256
PLANES = 24
CHUNKS = PLANES // ROWS
SPANS = ((0, 1), (1, 2))
XL = KX // COLS
KL = KZ // ROWS
POINTS_X = 3 * KX
POINTS_Z = 3 * KZ // 2
HALF_X = POINTS_X // 2
HALF_Z = POINTS_Z // 2
ZL = POINTS_Z // COLS
GROUPS = XL // 4
SLOTS = KL // 32
PART = SLOTS * GROUPS
F32 = jnp.float32
BF16 = jnp.bfloat16


def parts(table):
    table = np.asarray(table, np.float64)
    high = table.astype(np.float32).astype(ml_dtypes.bfloat16)
    low = (table - high.astype(np.float64)).astype(np.float32).astype(ml_dtypes.bfloat16)
    return [high, low]


def span_order():
    lane = np.arange(KZ)
    slot, rest = lane // (32 * ROWS), lane % (32 * ROWS)
    return (rest // 32) * KL + slot * 32 + rest % 32


def span_signed(modes):
    return np.where(modes < KZ // 2, modes, modes - KZ)


def stream_order():
    index = np.arange(KX)
    col, rest = index // XL, index % XL
    return col * XL + 4 * (rest % GROUPS) + rest // GROUPS


def span_angle(points):
    signed = span_signed(span_order())
    turn = np.mod((2 * points[:, None] + 1) * signed[None, :], 2 * POINTS_Z)
    return turn * (math.pi / POINTS_Z)


def span_inverse_tables():
    angle = span_angle(np.arange(HALF_Z))
    return parts(np.cos(angle)) + parts(np.sin(angle))


def span_forward_tables():
    main = (np.arange(8)[:, None] * ZL + np.arange(64)[None, :]).reshape(-1)
    tail = np.arange(8)[:, None, None] * ZL + 64 + np.arange(8)[None, None, :]
    tail = np.broadcast_to(tail, (8, 3, 8)).reshape(-1)
    points = np.concatenate([main, tail, np.zeros(64, np.int64)])
    used = (np.arange(points.size) < 704)[:, None]
    factor = used * (32.0 / POINTS_Z)
    angle = span_angle(points)
    return parts(np.cos(angle) * factor) + parts(np.sin(angle) * factor)


def stream_angle():
    turn = np.mod(stream_order()[:, None] * (2 * np.arange(HALF_X)[None, :] + 1), 2 * POINTS_X)
    return turn * (math.pi / POINTS_X)


def stream_inverse_tables():
    weight = np.where(stream_order() == 0, 1.0, 2.0)[:, None] / 32.0
    angle = stream_angle()
    return parts(weight * np.cos(angle)) + parts(-weight * np.sin(angle))


def stream_forward_tables():
    angle = stream_angle()
    return parts(np.cos(angle) / POINTS_X) + parts(-np.sin(angle) / POINTS_X)


def span_lanes():
    signed = span_signed(span_order())
    half = signed * (math.pi / POINTS_Z)
    rows = np.zeros((8, KZ), np.float32)
    rows[0] = np.cos(half)
    rows[1] = np.sin(half)
    return rows


def split(value):
    high = value.astype(BF16)
    low = (value - high.astype(F32)).astype(BF16)
    return high, low


def dot_nn(left, right):
    return lax.dot_general(left, right, (((1,), (0,)), ((), ())), preferred_element_type=F32)


def dot_nt(left, right):
    return lax.dot_general(left, right, (((1,), (1,)), ((), ())), preferred_element_type=F32)


def dot_tn(left, right):
    return lax.dot_general(left, right, (((0,), (0,)), ((), ())), preferred_element_type=F32)


def triple(dot, left, right):
    return dot(left[0], right[0]) + (dot(left[0], right[1]) + dot(left[1], right[0]))


def swap_blocks(tiles):
    lane = lax.broadcasted_iota(jnp.int32, tiles[0].shape, 1)
    low64 = lane < 64
    low32 = (lane & 32) == 0

    def turn(value, amount):
        return pltpu.roll(value, amount, 1)

    a0 = jnp.where(low64, tiles[0], turn(tiles[2], 64))
    a2 = jnp.where(low64, turn(tiles[0], 64), tiles[2])
    a1 = jnp.where(low64, tiles[1], turn(tiles[3], 64))
    a3 = jnp.where(low64, turn(tiles[1], 64), tiles[3])
    b0 = jnp.where(low32, a0, turn(a1, 32))
    b1 = jnp.where(low32, turn(a0, 96), a1)
    b2 = jnp.where(low32, a2, turn(a3, 32))
    b3 = jnp.where(low32, turn(a2, 96), a3)
    return [b0, b1, b2, b3]


def whole(shape):
    zeros = (0,) * len(shape)
    return pl.BlockSpec(shape, lambda *_: zeros)


def fixed(shape):
    zeros = (0,) * len(shape)
    return pl.BlockSpec(shape, lambda *_: zeros, pipeline_mode=pl.Buffered(1))


def in_hbm(shape):
    return pltpu.HBM(shape, F32)


def kept_in_hbm(value):
    return pltpu.with_memory_space_constraint(value, pltpu.HBM)


def params(megabytes):
    return pltpu.CompilerParams(
        dimension_semantics=("arbitrary",), vmem_limit_bytes=megabytes * 1024 * 1024
    )


PLANE_ROWS = 5 * 2 * PART
PLANE_STEP = 2


def plane_kernel(ops_ref, v_ref, g_ref, out_ref):
    zero = jnp.zeros((128 - 3 * PLANES, NY), F32)
    high, low = split(jnp.concatenate([ops_ref[...], zero], axis=0))
    both = jnp.concatenate([high, low], axis=0)
    for sub in range(PLANE_STEP):
        group = pl.program_id(0) * PLANE_STEP + sub

        def values(ref):
            pieces = []
            for c in range(2):
                for slot in range(SLOTS):
                    for t in range(4):
                        pieces.append(ref[c, 4 * sub + t, 32 * slot : 32 * slot + 32, :])
            rows_high, rows_low = split(jnp.concatenate(pieces, axis=0))
            first = dot_nt(rows_high, both)
            return jnp.transpose(first[:, :128] + (first[:, 128:] + dot_nt(rows_low, high)))

        v_values = values(v_ref)
        g_values = values(g_ref)
        for value in range(5):
            source = v_values if value < 3 else g_values
            first = (value if value < 3 else value - 3) * PLANES
            for chunk in range(CHUNKS):
                top = first + chunk * ROWS
                for c in range(2):
                    for slot in range(SLOTS):
                        lane = (c * SLOTS + slot) * 128
                        row = chunk * PLANE_ROWS + (value * 2 + c) * PART + slot * GROUPS + group
                        out_ref[pl.ds(row, ROWS, stride=CHUNKS * PLANE_ROWS), :] = source[
                            top : top + ROWS, lane : lane + 128
                        ]


def plane_values(plane_ops, v_coef, vort_coef):
    out = in_hbm((ROWS * CHUNKS * PLANE_ROWS, 128))
    coef = pl.BlockSpec((2, 4 * PLANE_STEP, KL, NY), lambda q: (0, q, 0, 0))
    return pl.pallas_call(
        plane_kernel,
        grid=(GROUPS // PLANE_STEP,),
        in_specs=[whole((3 * PLANES, NY)), coef, coef],
        out_specs=whole(out.shape),
        out_shape=out,
        compiler_params=params(24),
        name="plane_values",
    )(plane_ops.reshape(3 * PLANES, NY), kept_in_hbm(v_coef), kept_in_hbm(vort_coef))


def span_inverse_kernel(in_ref, wave_ref, lanes_ref, ch, cl, sh, sl, out_ref, dh, dl, eh, el):
    blocks = []
    for quad in range(ROWS // 4):
        blocks.append(swap_blocks([in_ref[4 * quad + i] for i in range(4)]))

    def value(index, c):
        top = (index * 2 + c) * PART
        rows = []
        for t in range(4):
            lanes = []
            for slot in range(SLOTS):
                at = top + slot * GROUPS
                for quad in range(ROWS // 4):
                    lanes.append(blocks[quad][t][at : at + GROUPS])
            rows.append(jnp.concatenate(lanes, axis=1))
        return jnp.concatenate(rows, axis=0)

    cosine = lanes_ref[0:1, :]
    sine = lanes_ref[1:2, :]

    def turned(index):
        re, im = value(index, 0), value(index, 1)
        return (re * cosine + im * sine, im * cosine - re * sine)

    v_base, v_slope, v_curve, g_base, g_slope = [turned(i) for i in range(5)]
    along, across = wave_ref[0], wave_ref[1]
    stream, span = wave_ref[2], wave_ref[3]

    def times_i(pair):
        return (-pair[1], pair[0])

    fields = [
        times_i([along * v_slope[c] - across * g_base[c] for c in range(2)]),
        v_base,
        times_i([across * v_slope[c] + along * g_base[c] for c in range(2)]),
        times_i(
            [across * v_curve[c] + along * g_slope[c] - span * v_base[c] for c in range(2)]
        ),
        g_base,
        times_i(
            [stream * v_base[c] - along * v_curve[c] + across * g_slope[c] for c in range(2)]
        ),
    ]
    for f, pair in enumerate(fields):
        top = f * 2 * XL
        re_high, re_low = split(pair[0])
        im_high, im_low = split(pair[1])
        dh[top : top + XL, :] = re_high
        dl[top : top + XL, :] = re_low
        dh[top + XL : top + 2 * XL, :] = im_high
        dl[top + XL : top + 2 * XL, :] = im_low
        eh[top : top + XL, :] = -im_high
        el[top : top + XL, :] = -im_low
        eh[top + XL : top + 2 * XL, :] = re_high
        el[top + XL : top + 2 * XL, :] = re_low
    straight = [dh[...], dl[...]]
    crossed = [eh[...], el[...]]
    even = triple(dot_nt, [ch[...], cl[...]], straight)
    odd = triple(dot_nt, [sh[...], sl[...]], crossed)
    for pair in range(COLS // 2):
        part = slice(pair * ZL, (pair + 1) * ZL)
        out_ref[2 * pair, 0] = even[part] + odd[part]
        out_ref[2 * pair + 1, 0] = even[part] - odd[part]


def span_inverse(received, first, count, wave, lanes, tables):
    out = in_hbm((COLS, count, ZL, 12 * XL))
    args = [wave, lanes] + tables
    return pl.pallas_call(
        span_inverse_kernel,
        grid=(count,),
        in_specs=[pl.BlockSpec((ROWS, PLANE_ROWS, 128), lambda p: (0, first + p, 0))]
        + [fixed(a.shape) for a in args],
        out_specs=pl.BlockSpec((COLS, 1, ZL, 12 * XL), lambda p: (0, p, 0, 0)),
        out_shape=out,
        scratch_shapes=[pltpu.VMEM((12 * XL, KZ), BF16)] * 4,
        compiler_params=params(24),
        name="span_inverse",
    )(received, *args)


BLOCK_X = 256


def product_kernel(in_ref, ch, cl, sh, sl, fch, fcl, fsh, fsl, out_ref, modes):
    for quad in range(COLS // 4):
        for column in range(3):
            tiles = [in_ref[4 * quad + i, 0, :, column * 128 : column * 128 + 128] for i in range(4)]
            for slot, tile in enumerate(swap_blocks(tiles)):
                top = (2 * column + slot // 2) * ZL
                modes[slot % 2, top : top + ZL, quad * 128 : quad * 128 + 128] = tile
    real = split(modes[0])
    imag = split(modes[1])
    total_re, total_im = None, None
    for block in range(HALF_X // BLOCK_X):
        here = slice(block * BLOCK_X, (block + 1) * BLOCK_X)
        even = triple(dot_nn, real, [ch[:, here], cl[:, here]])
        odd = triple(dot_nn, imag, [sh[:, here], sl[:, here]])

        def products(field):
            u, v, w, ox, oy, oz = [field[i * ZL : (i + 1) * ZL] for i in range(6)]
            return [v * oz - w * oy, w * ox - u * oz, u * oy - v * ox]

        right = products(even + odd)
        left = products(even - odd)

        def ordered(values):
            zeros = jnp.zeros((256 - 3 * ZL, BLOCK_X), F32)
            pieces = [x[:64] for x in values] + [x[64:] for x in values] + [zeros]
            return split(jnp.concatenate(pieces, axis=0))

        sums = ordered([r + l for r, l in zip(right, left)])
        gaps = ordered([r - l for r, l in zip(right, left)])
        part_re = triple(dot_nt, [fch[:, here], fcl[:, here]], sums)
        part_im = triple(dot_nt, [fsh[:, here], fsl[:, here]], gaps)
        total_re = part_re if total_re is None else total_re + part_re
        total_im = part_im if total_im is None else total_im + part_im
    for col in range(COLS):
        rows = slice(col * XL, (col + 1) * XL)
        out_ref[col, 0, 0] = total_re[rows]
        out_ref[col, 0, 1] = total_im[rows]


def stream_products(received, tables):
    count = received.shape[1]
    out = in_hbm((COLS, count, 2, XL, 256))
    return pl.pallas_call(
        product_kernel,
        grid=(count,),
        in_specs=[pl.BlockSpec((COLS, 1, ZL, 12 * XL), lambda p: (0, p, 0, 0))]
        + [fixed(a.shape) for a in tables],
        out_specs=pl.BlockSpec((COLS, 1, 2, XL, 256), lambda p: (0, p, 0, 0, 0)),
        out_shape=out,
        scratch_shapes=[pltpu.VMEM((2, 6 * ZL, KX), F32)],
        compiler_params=params(28),
        name="stream_products",
    )(received, *tables)


HOME_ROWS = 2 * 3 * PART


def span_forward_kernel(in_ref, lanes_ref, ch, cl, sh, sl, *rest):
    out_ref = rest[-1]
    sums, gaps = [], []
    for pair in range(8):
        plus = in_ref[2 * pair, 0].reshape(2 * XL, 256)
        minus = in_ref[2 * pair + 1, 0].reshape(2 * XL, 256)
        sums.append(plus + minus)
        gaps.append(plus - minus)
    lane = lax.broadcasted_iota(jnp.int32, (2 * XL, 128), 1)
    low64 = lane < 64

    def ordered(values):
        firsts = [x[:, :128] for x in values]
        lasts = [x[:, 128:] for x in values]
        main = [[], [], []]
        for i in range(0, 8, 2):
            a, b = firsts[i], firsts[i + 1]
            main[0].append(jnp.where(low64, a, pltpu.roll(b, 64, 1)))
            main[1].append(jnp.where(low64, pltpu.roll(a, 64, 1), b))
            main[2].append(jnp.where(low64, lasts[i], pltpu.roll(lasts[i + 1], 64, 1)))
        tails = [jnp.zeros_like(lasts[0]), jnp.zeros_like(lasts[0])]
        for i in range(8):
            start = 24 * i
            for half in range(2):
                low, high = max(start, 128 * half), min(start + 24, 128 * half + 128)
                if low >= high:
                    continue
                shift = (start - 64) % 128
                moved = pltpu.roll(lasts[i], shift, 1) if shift else lasts[i]
                inside = (lane >= low - 128 * half) & (lane < high - 128 * half)
                tails[half] = jnp.where(inside, moved, tails[half])
        out = []
        for h in range(3):
            ends = []
            for half in range(2):
                index = lane + 128 * half
                mine = ((index // 8) % 3 == h) & (index < 192)
                ends.append(jnp.where(mine, tails[half], 0.0))
            out.append(jnp.concatenate(main[h] + ends, axis=1))
        return out

    e_rows, o_rows = [], []
    even, odd = ordered(sums), ordered(gaps)
    for c in range(2):
        for h in range(3):
            e_rows.append(even[h][c * XL : (c + 1) * XL])
            o_rows.append(odd[h][XL:] if c == 0 else -odd[h][:XL])
    left = split(jnp.concatenate(e_rows, axis=0))
    right = split(jnp.concatenate(o_rows, axis=0))
    result = triple(dot_nn, left, [ch[...], cl[...]]) + triple(dot_nn, right, [sh[...], sl[...]])
    cosine = lanes_ref[0:1, :]
    sine = lanes_ref[1:2, :]
    re, im = result[: 3 * XL], result[3 * XL :]
    turned = [re * cosine - im * sine, re * sine + im * cosine]
    for c in range(2):
        for h in range(3):
            block = turned[c][h * XL : (h + 1) * XL]
            for slot in range(SLOTS):
                top = (c * 3 + h) * PART + slot * GROUPS
                for quad in range(ROWS // 4):
                    at = slot * 256 + quad * 128
                    tiles = [block[t * 8 : t * 8 + 8, at : at + 128] for t in range(4)]
                    for i, tile in enumerate(swap_blocks(tiles)):
                        out_ref[4 * quad + i, top : top + GROUPS, :] = tile


def span_forward(received, first, lanes, tables, earlier):
    count = received.shape[1]
    out = in_hbm((ROWS, CHUNKS * HOME_ROWS, 128))
    args = [lanes] + tables
    before = [] if earlier is None else [earlier]
    return pl.pallas_call(
        span_forward_kernel,
        grid=(count,),
        in_specs=[pl.BlockSpec((COLS, 1, 2, XL, 256), lambda p: (0, p, 0, 0, 0))]
        + [fixed(a.shape) for a in args]
        + [pl.BlockSpec(memory_space=pl.ANY)] * len(before),
        out_specs=pl.BlockSpec((ROWS, HOME_ROWS, 128), lambda p: (0, first + p, 0)),
        out_shape=out,
        input_output_aliases={1 + len(args): 0} if before else {},
        compiler_params=params(20),
        name="span_forward",
    )(received, *args, *before)


def combine_kernel(in_ref, factor_ref, inverse_ref, vort_ref, lapv_ref):
    group = pl.program_id(0)

    def stacked(value):
        high = value.astype(BF16).astype(F32)
        return high, value - high

    g_lanes, s_lanes = [], []
    for slot in range(SLOTS):
        factors = [factor_ref[i, pl.ds(slot * GROUPS + group, 1), :] for i in range(5)]

        def field(h, c):
            row = (c * 3 + h) * PART + slot * GROUPS + group
            return jnp.concatenate(
                [
                    in_ref[pl.ds(chunk * HOME_ROWS + row, ROWS, stride=CHUNKS * HOME_ROWS), :]
                    for chunk in range(CHUNKS)
                ],
                axis=0,
            )

        hx = [field(0, c) for c in range(2)]
        hy = [field(1, c) for c in range(2)]
        hz = [field(2, c) for c in range(2)]
        for c in range(2):
            other = 1 - c
            g_term = factors[0] * hx[other] - factors[1] * hz[other]
            s_term = factors[2] * hx[other] + factors[3] * hz[other]
            if c == 0:
                g_term = -g_term
            else:
                s_term = -s_term
            y_term = factors[4] * hy[c]
            gh, gl = stacked(g_term)
            sh, sl = stacked(s_term)
            yh, yl = stacked(y_term)
            g_lanes.append(jnp.concatenate([gh, gl, gh], axis=0))
            s_lanes.append(jnp.concatenate([sh, sl, sh, yh, yl, yh], axis=0))
    g_left = jnp.concatenate(g_lanes, axis=1).astype(BF16)
    s_left = jnp.concatenate(s_lanes, axis=1).astype(BF16)

    def right(index):
        high, low = stacked(inverse_ref[index])
        return jnp.concatenate([high, high, low], axis=0)

    first, second = right(0), right(1)
    vort = dot_tn(g_left, first.astype(BF16))
    lapv = dot_tn(s_left, jnp.concatenate([second, first], axis=0).astype(BF16))
    for slot in range(SLOTS):
        for c in range(2):
            for t in range(4):
                row = (slot * 2 + c) * 128 + t * 32
                vort_ref[c, t, 32 * slot : 32 * slot + 32, :] = vort[row : row + 32]
                lapv_ref[c, t, 32 * slot : 32 * slot + 32, :] = lapv[row : row + 32]


def combine_planes(received, factors, inverse_ops):
    out = in_hbm((2, XL, KL, NY))
    args = [received, factors, jnp.swapaxes(inverse_ops, 1, 2)]
    block = pl.BlockSpec((2, 4, KL, NY), lambda q: (0, q, 0, 0))
    return pl.pallas_call(
        combine_kernel,
        grid=(GROUPS,),
        in_specs=[fixed(a.shape) for a in args],
        out_specs=[block, block],
        out_shape=[out, out],
        compiler_params=params(24),
        name="combine_planes",
    )(*args)


def span_wave_arrays():
    row = jnp.arange(XL, dtype=jnp.int32)
    x = 4 * (row % GROUPS) + row // GROUPS + lax.axis_index("col") * XL
    stream = (STREAM_STEP * x.astype(F32))[:, None]
    signed = jnp.asarray(span_signed(span_order()), jnp.int32)
    span = (SPAN_STEP * signed.astype(F32))[None, :]
    square = stream * stream + span * span
    recip = 1.0 / jnp.where(square > 0, square, 1.0)
    full = jnp.zeros_like(square)
    return jnp.stack([stream * recip, span * recip, stream + full, span + full], axis=0)


def home_factors():
    part = jnp.arange(PART, dtype=jnp.int32)[:, None]
    lane = jnp.arange(128, dtype=jnp.int32)[None, :]
    x = 4 * (part % GROUPS) + lane // 32 + lax.axis_index("col") * XL
    k = 32 * (part // GROUPS) + lane % 32 + lax.axis_index("row") * KL
    stream = STREAM_STEP * x.astype(F32)
    span = SPAN_STEP * jnp.where(k < KZ // 2, k, k - KZ).astype(F32)
    square = stream * stream + span * span
    damp_g = 1.0 / jnp.sqrt(1.0 + square)
    damp_v = 1.0 / (1.0 + square)
    return jnp.stack(
        [damp_g * span, damp_g * stream, damp_v * stream, damp_v * span, -damp_v * square], axis=0
    )


def exchange(value, axis):
    return lax.all_to_all(value, axis, split_axis=0, concat_axis=0, tiled=True)


def per_device(v_coef, vort_coef, plane_ops, inverse_ops):
    def constants(arrays):
        return [kept_in_hbm(jnp.asarray(a)) for a in arrays]

    span_in = constants(span_inverse_tables())
    span_out = constants(span_forward_tables())
    stream = constants(stream_inverse_tables() + stream_forward_tables())
    lanes = jnp.asarray(span_lanes())
    wave = span_wave_arrays()
    factors = home_factors()
    values = plane_values(plane_ops, v_coef, vort_coef)
    pencils = exchange(values.reshape(ROWS, CHUNKS * PLANE_ROWS, 128), "row")
    spectral = None
    for first, count in SPANS:
        sent = span_inverse(pencils, first, count, wave, lanes, span_in)
        arrived = exchange(sent, "col")
        returned = exchange(stream_products(arrived, stream), "col")
        spectral = span_forward(returned, first, lanes, span_out, spectral)
    home = exchange(spectral, "row").reshape(ROWS * CHUNKS * HOME_ROWS, 128)
    vort_rhs, lapv_rhs = combine_planes(home, factors, inverse_ops)
    return (vort_rhs, lapv_rhs)


def solution(mesh):
    in_specs = (P(None, "col", "row", None), P(None, "col", "row", None), P(), P())
    out_specs = (P(None, "col", "row", None), P(None, "col", "row", None))
    return jax.shard_map(
        per_device, mesh=mesh, in_specs=in_specs, out_specs=out_specs, check_vma=False
    )
```

```python
import functools
import math

import jax
import jax.numpy as jnp
import ml_dtypes
import numpy as np
from jax import lax
from jax.experimental import pallas as pl
from jax.experimental.pallas import tpu as pltpu
from jax.sharding import PartitionSpec as P

STREAM_STEP = 0.25
SPAN_STEP = 2.0 / 3.0
ROWS = 8
COLS = 16
KX = 512
KZ = 768
NY = 256
PLANES = 24
CHUNKS = PLANES // ROWS
SPANS = ((2, 1), (0, 2))
XL = KX // COLS
KL = KZ // ROWS
POINTS_X = 3 * KX
POINTS_Z = 3 * KZ // 2
HALF_X = POINTS_X // 2
HALF_Z = POINTS_Z // 2
ZL = POINTS_Z // COLS
GROUPS = XL // 4
SLOTS = KL // 32
PART = SLOTS * GROUPS
F32 = jnp.float32
BF16 = jnp.bfloat16


def parts(table):
    table = np.asarray(table, np.float64)
    high = table.astype(np.float32).astype(ml_dtypes.bfloat16)
    low = (table - high.astype(np.float64)).astype(np.float32).astype(ml_dtypes.bfloat16)
    return [high, low]


def span_order():
    lane = np.arange(KZ)
    slot, rest = lane // (32 * ROWS), lane % (32 * ROWS)
    return (rest // 32) * KL + slot * 32 + rest % 32


def span_signed(modes):
    return np.where(modes < KZ // 2, modes, modes - KZ)


def stream_order():
    index = np.arange(KX)
    col, rest = index // XL, index % XL
    return col * XL + 4 * (rest % GROUPS) + rest // GROUPS


def span_angle(points):
    signed = span_signed(span_order())
    turn = np.mod((2 * points[:, None] + 1) * signed[None, :], 2 * POINTS_Z)
    return turn * (math.pi / POINTS_Z)


def span_inverse_tables():
    angle = span_angle(np.arange(HALF_Z))
    return parts(np.cos(angle)) + parts(np.sin(angle))


def span_forward_tables():
    main = (np.arange(8)[:, None] * ZL + np.arange(64)[None, :]).reshape(-1)
    tail = np.arange(8)[:, None, None] * ZL + 64 + np.arange(8)[None, None, :]
    tail = np.broadcast_to(tail, (8, 3, 8)).reshape(-1)
    points = np.concatenate([main, tail, np.zeros(64, np.int64)])
    used = (np.arange(points.size) < 704)[:, None]
    factor = used * (32.0 / POINTS_Z)
    angle = span_angle(points)
    return parts(np.cos(angle) * factor) + parts(np.sin(angle) * factor)


def stream_angle():
    turn = np.mod(stream_order()[:, None] * (2 * np.arange(HALF_X)[None, :] + 1), 2 * POINTS_X)
    return turn * (math.pi / POINTS_X)


def stream_inverse_tables():
    weight = np.where(stream_order() == 0, 1.0, 2.0)[:, None] / 32.0
    angle = stream_angle()
    return parts(weight * np.cos(angle)) + parts(-weight * np.sin(angle))


def stream_forward_tables():
    angle = stream_angle()
    return parts(np.cos(angle) / POINTS_X) + parts(-np.sin(angle) / POINTS_X)


def span_lanes():
    signed = span_signed(span_order())
    half = signed * (math.pi / POINTS_Z)
    rows = np.zeros((8, KZ), np.float32)
    rows[0] = np.cos(half)
    rows[1] = np.sin(half)
    return rows


def split(value):
    high = value.astype(BF16)
    low = (value - high.astype(F32)).astype(BF16)
    return high, low


def dot_nn(left, right):
    return lax.dot_general(left, right, (((1,), (0,)), ((), ())), preferred_element_type=F32)


def dot_nt(left, right):
    return lax.dot_general(left, right, (((1,), (1,)), ((), ())), preferred_element_type=F32)


def dot_tn(left, right):
    return lax.dot_general(left, right, (((0,), (0,)), ((), ())), preferred_element_type=F32)


def triple(dot, left, right):
    return dot(left[0], right[0]) + (dot(left[0], right[1]) + dot(left[1], right[0]))


def swap_blocks(tiles):
    lane = lax.broadcasted_iota(jnp.int32, tiles[0].shape, 1)
    low64 = lane < 64
    low32 = (lane & 32) == 0

    def turn(value, amount):
        return pltpu.roll(value, amount, 1)

    a0 = jnp.where(low64, tiles[0], turn(tiles[2], 64))
    a2 = jnp.where(low64, turn(tiles[0], 64), tiles[2])
    a1 = jnp.where(low64, tiles[1], turn(tiles[3], 64))
    a3 = jnp.where(low64, turn(tiles[1], 64), tiles[3])
    b0 = jnp.where(low32, a0, turn(a1, 32))
    b1 = jnp.where(low32, turn(a0, 96), a1)
    b2 = jnp.where(low32, a2, turn(a3, 32))
    b3 = jnp.where(low32, turn(a2, 96), a3)
    return [b0, b1, b2, b3]


def whole(shape):
    zeros = (0,) * len(shape)
    return pl.BlockSpec(shape, lambda *_: zeros)


def fixed(shape):
    zeros = (0,) * len(shape)
    return pl.BlockSpec(shape, lambda *_: zeros, pipeline_mode=pl.Buffered(1))


def in_hbm(shape):
    return pltpu.HBM(shape, F32)


def kept_in_hbm(value):
    return pltpu.with_memory_space_constraint(value, pltpu.HBM)


def params(megabytes):
    return pltpu.CompilerParams(
        dimension_semantics=("arbitrary",), vmem_limit_bytes=megabytes * 1024 * 1024
    )


PLANE_ROWS = 5 * 2 * PART
PLANE_STEP = 2


def plane_kernel(ops_ref, v_ref, g_ref, out_ref):
    zero = jnp.zeros((128 - 3 * PLANES, NY), F32)
    high, low = split(jnp.concatenate([ops_ref[...], zero], axis=0))
    both = jnp.concatenate([high, low], axis=0)
    for sub in range(PLANE_STEP):
        group = pl.program_id(0) * PLANE_STEP + sub

        def values(ref):
            pieces = []
            for c in range(2):
                for slot in range(SLOTS):
                    for t in range(4):
                        pieces.append(ref[c, 4 * sub + t, 32 * slot : 32 * slot + 32, :])
            rows_high, rows_low = split(jnp.concatenate(pieces, axis=0))
            first = dot_nt(rows_high, both)
            return jnp.transpose(first[:, :128] + (first[:, 128:] + dot_nt(rows_low, high)))

        v_values = values(v_ref)
        g_values = values(g_ref)
        for value in range(5):
            source = v_values if value < 3 else g_values
            first = (value if value < 3 else value - 3) * PLANES
            for chunk in range(CHUNKS):
                top = first + chunk * ROWS
                for c in range(2):
                    for slot in range(SLOTS):
                        lane = (c * SLOTS + slot) * 128
                        row = chunk * PLANE_ROWS + (value * 2 + c) * PART + slot * GROUPS + group
                        out_ref[pl.ds(row, ROWS, stride=CHUNKS * PLANE_ROWS), :] = source[
                            top : top + ROWS, lane : lane + 128
                        ]


def plane_values(plane_ops, v_coef, vort_coef):
    out = in_hbm((ROWS * CHUNKS * PLANE_ROWS, 128))
    coef = pl.BlockSpec((2, 4 * PLANE_STEP, KL, NY), lambda q: (0, q, 0, 0))
    return pl.pallas_call(
        plane_kernel,
        grid=(GROUPS // PLANE_STEP,),
        in_specs=[whole((3 * PLANES, NY)), coef, coef],
        out_specs=whole(out.shape),
        out_shape=out,
        compiler_params=params(24),
        name="plane_values",
    )(kept_in_hbm(plane_ops.reshape(3 * PLANES, NY)), kept_in_hbm(v_coef), kept_in_hbm(vort_coef))


SPAN_STEPS = 1


def span_inverse_kernel(count, in_ref, wave_ref, lanes_ref, ch, cl, sh, sl, out_ref, *scratch):
    dh, dl, eh, el = scratch

    @pl.when(pl.program_id(0) == 0)
    def _():
        for plane in range(count):
            span_fields(plane, in_ref, wave_ref, lanes_ref, dh, dl, eh, el)

    even = triple(dot_nt, [ch[...], cl[...]], [dh[...], dl[...]])
    odd = triple(dot_nt, [sh[...], sl[...]], [eh[...], el[...]])
    for pair in range(COLS // 2 // SPAN_STEPS):
        part = slice(pair * ZL, (pair + 1) * ZL)
        for plane in range(count):
            lanes = slice(plane * 12 * XL, (plane + 1) * 12 * XL)
            out_ref[2 * pair, plane] = even[part, lanes] + odd[part, lanes]
            out_ref[2 * pair + 1, plane] = even[part, lanes] - odd[part, lanes]


def span_fields(plane, in_ref, wave_ref, lanes_ref, dh, dl, eh, el):
    mine = slice(plane * PLANE_ROWS, (plane + 1) * PLANE_ROWS)
    blocks = []
    for quad in range(ROWS // 4):
        blocks.append(swap_blocks([in_ref[4 * quad + i, mine] for i in range(4)]))

    def value(index, c):
        top = (index * 2 + c) * PART
        rows = []
        for t in range(4):
            lanes = []
            for slot in range(SLOTS):
                at = top + slot * GROUPS
                for quad in range(ROWS // 4):
                    lanes.append(blocks[quad][t][at : at + GROUPS])
            rows.append(jnp.concatenate(lanes, axis=1))
        return jnp.concatenate(rows, axis=0)

    cosine = lanes_ref[0:1, :]
    sine = lanes_ref[1:2, :]

    def turned(index):
        re, im = value(index, 0), value(index, 1)
        return (re * cosine + im * sine, im * cosine - re * sine)

    v_base, v_slope, v_curve, g_base, g_slope = [turned(i) for i in range(5)]
    along, across = wave_ref[0], wave_ref[1]
    stream, span = wave_ref[2], wave_ref[3]

    def times_i(pair):
        return (-pair[1], pair[0])

    fields = [
        times_i([along * v_slope[c] - across * g_base[c] for c in range(2)]),
        v_base,
        times_i([across * v_slope[c] + along * g_base[c] for c in range(2)]),
        times_i(
            [across * v_curve[c] + along * g_slope[c] - span * v_base[c] for c in range(2)]
        ),
        g_base,
        times_i(
            [stream * v_base[c] - along * v_curve[c] + across * g_slope[c] for c in range(2)]
        ),
    ]
    for f, pair in enumerate(fields):
        top = (plane * 6 + f) * 2 * XL
        re_high, re_low = split(pair[0])
        im_high, im_low = split(pair[1])
        dh[top : top + XL, :] = re_high
        dl[top : top + XL, :] = re_low
        dh[top + XL : top + 2 * XL, :] = im_high
        dl[top + XL : top + 2 * XL, :] = im_low
        eh[top : top + XL, :] = -im_high
        el[top : top + XL, :] = -im_low
        eh[top + XL : top + 2 * XL, :] = re_high
        el[top + XL : top + 2 * XL, :] = re_low


def span_inverse(received, first, count, wave, lanes, tables):
    out = in_hbm((COLS, count, ZL, 12 * XL))
    args = [wave, lanes]
    rows = HALF_Z // SPAN_STEPS
    return pl.pallas_call(
        functools.partial(span_inverse_kernel, count),
        grid=(SPAN_STEPS,),
        in_specs=[pl.BlockSpec((ROWS, count * PLANE_ROWS, 128), lambda j: (0, first // count, 0))]
        + [fixed(a.shape) for a in args]
        + [fixed((rows, KZ))] * 4,
        out_specs=pl.BlockSpec((COLS // SPAN_STEPS, count, ZL, 12 * XL), lambda j: (j, 0, 0, 0)),
        out_shape=out,
        scratch_shapes=[pltpu.VMEM((count * 12 * XL, KZ), BF16)] * 4,
        compiler_params=params(32),
        name="span_inverse",
    )(received, *args, *tables)


BLOCK_X = 256


def product_kernel(count, in_ref, ch, cl, sh, sl, fch, fcl, fsh, fsl, out_ref, modes):
    for quad in range(COLS // 4):
        for column in range(3):
            tiles = [in_ref[4 * quad + i, 0, :, column * 128 : column * 128 + 128] for i in range(4)]
            for slot, tile in enumerate(swap_blocks(tiles)):
                top = (2 * column + slot // 2) * ZL
                modes[slot % 2, top : top + ZL, quad * 128 : quad * 128 + 128] = tile
    real = split(modes[0])
    imag = split(modes[1])
    total_re, total_im = None, None
    for block in range(HALF_X // BLOCK_X):
        here = slice(block * BLOCK_X, (block + 1) * BLOCK_X)
        even = triple(dot_nn, real, [ch[:, here], cl[:, here]])
        odd = triple(dot_nn, imag, [sh[:, here], sl[:, here]])

        def products(field):
            u, v, w, ox, oy, oz = [field[i * ZL : (i + 1) * ZL] for i in range(6)]
            return [v * oz - w * oy, w * ox - u * oz, u * oy - v * ox]

        right = products(even + odd)
        left = products(even - odd)

        def ordered(values):
            zeros = jnp.zeros((256 - 3 * ZL, BLOCK_X), F32)
            pieces = [x[:64] for x in values] + [x[64:] for x in values] + [zeros]
            return split(jnp.concatenate(pieces, axis=0))

        sums = ordered([r + l for r, l in zip(right, left)])
        gaps = ordered([r - l for r, l in zip(right, left)])
        part_re = triple(dot_nt, [fch[:, here], fcl[:, here]], sums)
        part_im = triple(dot_nt, [fsh[:, here], fsl[:, here]], gaps)
        total_re = part_re if total_re is None else total_re + part_re
        total_im = part_im if total_im is None else total_im + part_im
    lane = lax.broadcasted_iota(jnp.int32, (KX, 128), 1)
    last_re, last_im = total_re[:, 128:], total_im[:, 128:]
    third = jnp.where(lane < 64, last_re, pltpu.roll(last_im, 64, 1))
    ends = jnp.where(lane < 24, pltpu.roll(last_re, 64, 1), pltpu.roll(last_im, 88, 1))
    lane3 = lax.broadcasted_iota(jnp.int32, (COLS, XL, 128), 2)
    tail = slice(384 * count, 384 * count + 128)
    for plane in range(count):

        @pl.when(pl.program_id(0) == plane)
        def _():
            at = 384 * plane
            out_ref[:, :, at : at + 128] = total_re[:, :128].reshape(COLS, XL, 128)
            out_ref[:, :, at + 128 : at + 256] = total_im[:, :128].reshape(COLS, XL, 128)
            out_ref[:, :, at + 256 : at + 384] = third.reshape(COLS, XL, 128)
            if plane == 0:
                out_ref[:, :, tail] = jnp.where(lane3 < 48, ends.reshape(COLS, XL, 128), 0.0)
            else:
                moved = jnp.where(lane < 96, pltpu.roll(ends, 48, 1), 0.0).reshape(COLS, XL, 128)
                out_ref[:, :, tail] = jnp.where(lane3 < 48, out_ref[:, :, tail], moved)


def stream_products(received, tables):
    count = received.shape[1]
    out = in_hbm((COLS, XL, 384 * count + 128))
    return pl.pallas_call(
        functools.partial(product_kernel, count),
        grid=(count,),
        in_specs=[pl.BlockSpec((COLS, 1, ZL, 12 * XL), lambda p: (0, p, 0, 0))]
        + [fixed(a.shape) for a in tables],
        out_specs=whole(out.shape),
        out_shape=out,
        scratch_shapes=[pltpu.VMEM((2, 6 * ZL, KX), F32)],
        compiler_params=params(32),
        name="stream_products",
    )(received, *tables)


HOME_ROWS = 2 * 3 * PART


def span_forward_kernel(count, in_ref, lanes_ref, ch, cl, sh, sl, *rest):
    out_ref, left_high, left_low, right_high, right_low = rest[-5:]

    for plane in range(count):
        e_rows, o_rows = span_pairs(in_ref, plane, count)
        rows = slice(plane * 6 * XL, (plane + 1) * 6 * XL)
        left_high[rows], left_low[rows] = split(jnp.concatenate(e_rows, axis=0))
        right_high[rows], right_low[rows] = split(jnp.concatenate(o_rows, axis=0))

    result = triple(dot_nn, [left_high[...], left_low[...]], [ch[...], cl[...]]) + triple(
        dot_nn, [right_high[...], right_low[...]], [sh[...], sl[...]]
    )
    cosine = lanes_ref[0:1, :]
    sine = lanes_ref[1:2, :]
    for plane in range(count):
        top = plane * 6 * XL
        re, im = result[top : top + 3 * XL], result[top + 3 * XL : top + 6 * XL]
        turned = [re * cosine - im * sine, re * sine + im * cosine]
        for c in range(2):
            for h in range(3):
                block = turned[c][h * XL : (h + 1) * XL]
                row = plane * 6 * GROUPS + (c * 3 + h) * GROUPS
                for slot in range(SLOTS):
                    for quad in range(ROWS // 4):
                        at = slot * 256 + quad * 128
                        tiles = [block[t * 8 : t * 8 + 8, at : at + 128] for t in range(4)]
                        for i, tile in enumerate(swap_blocks(tiles)):
                            out_ref[4 * quad + i, slot, row : row + GROUPS, :] = tile


def span_pairs(in_ref, plane, count):
    lane = lax.broadcasted_iota(jnp.int32, (XL, 128), 1)
    low64 = lane < 64
    at = 384 * plane

    def pieces(index):
        offsets = [at, at + 128, at + 256, 384 * count]
        return [in_ref[index, :, o : o + 128] for o in offsets]

    sums, gaps = [], []
    for pair in range(8):
        plus, minus = pieces(2 * pair), pieces(2 * pair + 1)
        sums.append([p + m for p, m in zip(plus, minus)])
        gaps.append([p - m for p, m in zip(plus, minus)])

    def turn(value, amount):
        amount = amount % 128
        return pltpu.roll(value, amount, 1) if amount else value

    def ordered(values, c):
        main = [[], [], []]
        for i in range(0, 8, 2):
            a, b = values[i][c], values[i + 1][c]
            main[0].append(jnp.where(low64, a, turn(b, 64)))
            main[1].append(jnp.where(low64, turn(a, 64), b))
            a, b = values[i][2], values[i + 1][2]
            if c == 0:
                main[2].append(jnp.where(low64, a, turn(b, 64)))
            else:
                main[2].append(jnp.where(low64, turn(a, 64), b))
        tails = [None, None]
        for i in range(8):
            start = 24 * i
            moved = turn(values[i][3], start - 24 * (2 * plane + c))
            for half in range(2):
                low, high = max(start - 128 * half, 0), min(start + 24 - 128 * half, 128)
                if low >= high:
                    continue
                inside = (lane >= low) & (lane < high)
                rest = jnp.zeros_like(moved) if tails[half] is None else tails[half]
                tails[half] = jnp.where(inside, moved, rest)
        out = []
        for h in range(3):
            ends = []
            for half in range(2):
                index = lane + 128 * half
                mine = ((index // 8) % 3 == h) & (index < 192)
                ends.append(jnp.where(mine, tails[half], 0.0))
            out.append(jnp.concatenate(main[h] + ends, axis=1))
        return out

    even = ordered(sums, 0) + ordered(sums, 1)
    odd = ordered(gaps, 1) + [-x for x in ordered(gaps, 0)]
    return even, odd


def span_forward(received, first, count, lanes, tables, earlier):
    out = in_hbm((ROWS, SLOTS, CHUNKS * 6 * GROUPS, 128))
    before = [] if earlier is None else [earlier]
    return pl.pallas_call(
        functools.partial(span_forward_kernel, count),
        grid=(1,),
        in_specs=[fixed(received.shape), fixed(lanes.shape)]
        + [fixed((KZ, KZ))] * 4
        + [pl.BlockSpec(memory_space=pl.ANY)] * len(before),
        out_specs=pl.BlockSpec(
            (ROWS, SLOTS, count * 6 * GROUPS, 128), lambda s: (0, 0, first // count, 0)
        ),
        out_shape=out,
        scratch_shapes=[pltpu.VMEM((count * 6 * XL, KZ), BF16)] * 4,
        input_output_aliases={2 + len(tables): 0} if before else {},
        compiler_params=params(20),
        name="span_forward",
    )(received, lanes, *tables, *before)


COMBINE_STEP = 2


def combine_kernel(in_ref, factor_ref, inverse_ref, vort_ref, lapv_ref):
    def stacked(value):
        high = value.astype(BF16).astype(F32)
        return high, value - high

    def right(index):
        high, low = stacked(inverse_ref[index])
        return jnp.concatenate([high, high, low], axis=0)

    first, second = right(0), right(1)
    both = jnp.concatenate([second, first], axis=0).astype(BF16)
    first = first.astype(BF16)
    for sub in range(COMBINE_STEP):
        group = pl.program_id(0) * COMBINE_STEP + sub
        g_lanes, s_lanes = [], []
        for slot in range(SLOTS):
            factors = [factor_ref[i, pl.ds(slot * GROUPS + group, 1), :] for i in range(5)]

            def field(h, c):
                row = slot * CHUNKS * 6 * GROUPS + (c * 3 + h) * GROUPS + group
                return jnp.concatenate(
                    [
                        in_ref[pl.ds(chunk * 6 * GROUPS + row, ROWS, stride=CHUNKS * HOME_ROWS), :]
                        for chunk in range(CHUNKS)
                    ],
                    axis=0,
                )

            hx = [field(0, c) for c in range(2)]
            hy = [field(1, c) for c in range(2)]
            hz = [field(2, c) for c in range(2)]
            for c in range(2):
                other = 1 - c
                g_term = factors[0] * hx[other] - factors[1] * hz[other]
                s_term = factors[2] * hx[other] + factors[3] * hz[other]
                if c == 0:
                    g_term = -g_term
                else:
                    s_term = -s_term
                y_term = factors[4] * hy[c]
                gh, gl = stacked(g_term)
                sh, sl = stacked(s_term)
                yh, yl = stacked(y_term)
                g_lanes.append(jnp.concatenate([gh, gl, gh], axis=0))
                s_lanes.append(jnp.concatenate([sh, sl, sh, yh, yl, yh], axis=0))
        g_left = jnp.concatenate(g_lanes, axis=1).astype(BF16)
        s_left = jnp.concatenate(s_lanes, axis=1).astype(BF16)
        vort = dot_tn(g_left, first)
        lapv = dot_tn(s_left, both)
        for slot in range(SLOTS):
            for c in range(2):
                for t in range(4):
                    row = (slot * 2 + c) * 128 + t * 32
                    vort_ref[c, 4 * sub + t, 32 * slot : 32 * slot + 32, :] = vort[row : row + 32]
                    lapv_ref[c, 4 * sub + t, 32 * slot : 32 * slot + 32, :] = lapv[row : row + 32]


def combine_planes(received, factors, inverse_ops):
    out = in_hbm((2, XL, KL, NY))
    args = [received, factors, jnp.swapaxes(inverse_ops, 1, 2)]
    block = pl.BlockSpec((2, 4 * COMBINE_STEP, KL, NY), lambda q: (0, q, 0, 0))
    return pl.pallas_call(
        combine_kernel,
        grid=(GROUPS // COMBINE_STEP,),
        in_specs=[fixed(a.shape) for a in args],
        out_specs=[block, block],
        out_shape=[out, out],
        compiler_params=params(24),
        name="combine_planes",
    )(*args)


def span_wave_arrays():
    row = jnp.arange(XL, dtype=jnp.int32)
    x = 4 * (row % GROUPS) + row // GROUPS + lax.axis_index("col") * XL
    stream = (STREAM_STEP * x.astype(F32))[:, None]
    signed = jnp.asarray(span_signed(span_order()), jnp.int32)
    span = (SPAN_STEP * signed.astype(F32))[None, :]
    square = stream * stream + span * span
    recip = 1.0 / jnp.where(square > 0, square, 1.0)
    full = jnp.zeros_like(square)
    return jnp.stack([stream * recip, span * recip, stream + full, span + full], axis=0)


def home_factors():
    part = jnp.arange(PART, dtype=jnp.int32)[:, None]
    lane = jnp.arange(128, dtype=jnp.int32)[None, :]
    x = 4 * (part % GROUPS) + lane // 32 + lax.axis_index("col") * XL
    k = 32 * (part // GROUPS) + lane % 32 + lax.axis_index("row") * KL
    stream = STREAM_STEP * x.astype(F32)
    span = SPAN_STEP * jnp.where(k < KZ // 2, k, k - KZ).astype(F32)
    square = stream * stream + span * span
    damp_g = 1.0 / jnp.sqrt(1.0 + square)
    damp_v = 1.0 / (1.0 + square)
    return jnp.stack(
        [damp_g * span, damp_g * stream, damp_v * stream, damp_v * span, -damp_v * square], axis=0
    )


def exchange(value, axis):
    return lax.all_to_all(value, axis, split_axis=0, concat_axis=0, tiled=True)


def per_device(v_coef, vort_coef, plane_ops, inverse_ops):
    def constants(arrays):
        return [kept_in_hbm(jnp.asarray(a)) for a in arrays]

    span_in = constants(span_inverse_tables())
    span_out = constants(span_forward_tables())
    stream = constants(stream_inverse_tables() + stream_forward_tables())
    lanes = jnp.asarray(span_lanes())
    wave = span_wave_arrays()
    factors = home_factors()
    values = plane_values(plane_ops, v_coef, vort_coef)
    pencils = exchange(values.reshape(ROWS, CHUNKS * PLANE_ROWS, 128), "row")
    spectral = None
    for first, count in SPANS:
        sent = span_inverse(pencils, first, count, wave, lanes, span_in)
        arrived = exchange(sent, "col")
        returned = exchange(stream_products(arrived, stream), "col")
        spectral = span_forward(returned, first, count, lanes, span_out, spectral)
    home = exchange(spectral.reshape(ROWS, CHUNKS * HOME_ROWS, 128), "row")
    home = home.reshape(ROWS * CHUNKS * HOME_ROWS, 128)
    vort_rhs, lapv_rhs = combine_planes(home, factors, inverse_ops)
    return (vort_rhs, lapv_rhs)


def solution(mesh):
    in_specs = (P(None, "col", "row", None), P(None, "col", "row", None), P(), P())
    out_specs = (P(None, "col", "row", None), P(None, "col", "row", None))
    return jax.shard_map(
        per_device, mesh=mesh, in_specs=in_specs, out_specs=out_specs, check_vma=False
    )
```

```python
import functools
import math

import jax
import jax.numpy as jnp
import ml_dtypes
import numpy as np
from jax import lax
from jax.experimental import pallas as pl
from jax.experimental.pallas import tpu as pltpu
from jax.sharding import PartitionSpec as P

STREAM_STEP = 0.25
SPAN_STEP = 2.0 / 3.0
ROWS = 8
COLS = 16
KX = 512
KZ = 768
NY = 256
PLANES = 24
CHUNKS = PLANES // ROWS
SPANS = ((2, 1), (0, 2))
XL = KX // COLS
KL = KZ // ROWS
POINTS_X = 3 * KX
POINTS_Z = 3 * KZ // 2
HALF_X = POINTS_X // 2
HALF_Z = POINTS_Z // 2
ZL = POINTS_Z // COLS
GROUPS = XL // 4
SLOTS = KL // 32
PART = SLOTS * GROUPS
F32 = jnp.float32
BF16 = jnp.bfloat16


def parts(table):
    table = np.asarray(table, np.float64)
    high = table.astype(np.float32).astype(ml_dtypes.bfloat16)
    low = (table - high.astype(np.float64)).astype(np.float32).astype(ml_dtypes.bfloat16)
    return [high, low]


def span_order():
    lane = np.arange(KZ)
    slot, rest = lane // (32 * ROWS), lane % (32 * ROWS)
    return (rest // 32) * KL + slot * 32 + rest % 32


def span_signed(modes):
    return np.where(modes < KZ // 2, modes, modes - KZ)


def stream_order():
    index = np.arange(KX)
    col, rest = index // XL, index % XL
    return col * XL + 4 * (rest % GROUPS) + rest // GROUPS


def span_angle(points):
    signed = span_signed(span_order())
    turn = np.mod((2 * points[:, None] + 1) * signed[None, :], 2 * POINTS_Z)
    return turn * (math.pi / POINTS_Z)


def span_inverse_tables():
    angle = span_angle(np.arange(HALF_Z))
    return parts(np.cos(angle)) + parts(np.sin(angle))


def span_forward_tables():
    main = (np.arange(8)[:, None] * ZL + np.arange(64)[None, :]).reshape(-1)
    tail = np.arange(8)[:, None, None] * ZL + 64 + np.arange(8)[None, None, :]
    tail = np.broadcast_to(tail, (8, 3, 8)).reshape(-1)
    points = np.concatenate([main, tail, np.zeros(64, np.int64)])
    used = (np.arange(points.size) < 704)[:, None]
    factor = used * (32.0 / POINTS_Z)
    angle = span_angle(points)
    return parts(np.cos(angle) * factor) + parts(np.sin(angle) * factor)


def stream_angle():
    turn = np.mod(stream_order()[:, None] * (2 * np.arange(HALF_X)[None, :] + 1), 2 * POINTS_X)
    return turn * (math.pi / POINTS_X)


def stream_inverse_tables():
    weight = np.where(stream_order() == 0, 1.0, 2.0)[:, None] / 32.0
    angle = stream_angle()
    return parts(weight * np.cos(angle)) + parts(-weight * np.sin(angle))


def stream_forward_tables():
    angle = stream_angle()
    return parts(np.cos(angle) / POINTS_X) + parts(-np.sin(angle) / POINTS_X)


def span_lanes():
    signed = span_signed(span_order())
    half = signed * (math.pi / POINTS_Z)
    rows = np.zeros((8, KZ), np.float32)
    rows[0] = np.cos(half)
    rows[1] = np.sin(half)
    return rows


def split(value):
    high = value.astype(BF16)
    low = (value - high.astype(F32)).astype(BF16)
    return high, low


def dot_nn(left, right):
    return lax.dot_general(left, right, (((1,), (0,)), ((), ())), preferred_element_type=F32)


def dot_nt(left, right):
    return lax.dot_general(left, right, (((1,), (1,)), ((), ())), preferred_element_type=F32)


def dot_tn(left, right):
    return lax.dot_general(left, right, (((0,), (0,)), ((), ())), preferred_element_type=F32)


def triple(dot, left, right):
    return dot(left[0], right[0]) + (dot(left[0], right[1]) + dot(left[1], right[0]))


def swap_blocks(tiles):
    lane = lax.broadcasted_iota(jnp.int32, tiles[0].shape, 1)
    low64 = lane < 64
    low32 = (lane & 32) == 0

    def turn(value, amount):
        return pltpu.roll(value, amount, 1)

    a0 = jnp.where(low64, tiles[0], turn(tiles[2], 64))
    a2 = jnp.where(low64, turn(tiles[0], 64), tiles[2])
    a1 = jnp.where(low64, tiles[1], turn(tiles[3], 64))
    a3 = jnp.where(low64, turn(tiles[1], 64), tiles[3])
    b0 = jnp.where(low32, a0, turn(a1, 32))
    b1 = jnp.where(low32, turn(a0, 96), a1)
    b2 = jnp.where(low32, a2, turn(a3, 32))
    b3 = jnp.where(low32, turn(a2, 96), a3)
    return [b0, b1, b2, b3]


def whole(shape):
    zeros = (0,) * len(shape)
    return pl.BlockSpec(shape, lambda *_: zeros)


def fixed(shape):
    zeros = (0,) * len(shape)
    return pl.BlockSpec(shape, lambda *_: zeros, pipeline_mode=pl.Buffered(1))


def on_chip():
    return pl.BlockSpec(memory_space=pltpu.VMEM)


def in_hbm(shape):
    return pltpu.HBM(shape, F32)


def kept_in_hbm(value):
    return pltpu.with_memory_space_constraint(value, pltpu.HBM)


def params(megabytes):
    return pltpu.CompilerParams(
        dimension_semantics=("arbitrary",), vmem_limit_bytes=megabytes * 1024 * 1024
    )


PLANE_ROWS = 5 * 2 * PART
PLANE_STEP = 4


def plane_kernel(ops_ref, v_ref, g_ref, out_ref):
    zero = jnp.zeros((128 - 3 * PLANES, NY), F32)
    high, low = split(jnp.concatenate([ops_ref[...], zero], axis=0))
    both = jnp.concatenate([high, low], axis=0)
    for sub in range(PLANE_STEP):
        group = pl.program_id(0) * PLANE_STEP + sub

        def values(ref):
            pieces = []
            for c in range(2):
                for slot in range(SLOTS):
                    for t in range(4):
                        pieces.append(ref[c, 4 * sub + t, 32 * slot : 32 * slot + 32, :])
            rows_high, rows_low = split(jnp.concatenate(pieces, axis=0))
            first = dot_nt(rows_high, both)
            return jnp.transpose(first[:, :128] + (first[:, 128:] + dot_nt(rows_low, high)))

        v_values = values(v_ref)
        g_values = values(g_ref)
        for value in range(5):
            source = v_values if value < 3 else g_values
            first = (value if value < 3 else value - 3) * PLANES
            for chunk in range(CHUNKS):
                top = first + chunk * ROWS
                for c in range(2):
                    for slot in range(SLOTS):
                        lane = (c * SLOTS + slot) * 128
                        row = chunk * PLANE_ROWS + (value * 2 + c) * PART + slot * GROUPS + group
                        out_ref[pl.ds(row, ROWS, stride=CHUNKS * PLANE_ROWS), :] = source[
                            top : top + ROWS, lane : lane + 128
                        ]


def plane_values(plane_ops, v_coef, vort_coef):
    out = in_hbm((ROWS * CHUNKS * PLANE_ROWS, 128))
    coef = pl.BlockSpec((2, 4 * PLANE_STEP, KL, NY), lambda q: (0, q, 0, 0))
    return pl.pallas_call(
        plane_kernel,
        grid=(GROUPS // PLANE_STEP,),
        in_specs=[whole((3 * PLANES, NY)), coef, coef],
        out_specs=whole(out.shape),
        out_shape=out,
        compiler_params=params(44),
        name="plane_values",
    )(kept_in_hbm(plane_ops.reshape(3 * PLANES, NY)), kept_in_hbm(v_coef), kept_in_hbm(vort_coef))


SPAN_STEPS = 1


def span_inverse_kernel(first, count, in_ref, wave_ref, lanes_ref, ch, cl, sh, sl, out_ref, *scratch):
    dh, dl, eh, el = scratch

    @pl.when(pl.program_id(0) == 0)
    def _():
        for plane in range(count):
            span_fields(first, plane, in_ref, wave_ref, lanes_ref, dh, dl, eh, el)

    even = triple(dot_nt, [ch[...], cl[...]], [dh[...], dl[...]])
    odd = triple(dot_nt, [sh[...], sl[...]], [eh[...], el[...]])
    for pair in range(COLS // 2 // SPAN_STEPS):
        part = slice(pair * ZL, (pair + 1) * ZL)
        for plane in range(count):
            lanes = slice(plane * 12 * XL, (plane + 1) * 12 * XL)
            out_ref[2 * pair, plane] = even[part, lanes] + odd[part, lanes]
            out_ref[2 * pair + 1, plane] = even[part, lanes] - odd[part, lanes]


def span_fields(first, plane, in_ref, wave_ref, lanes_ref, dh, dl, eh, el):
    mine = slice((first + plane) * PLANE_ROWS, (first + plane + 1) * PLANE_ROWS)
    blocks = []
    for quad in range(ROWS // 4):
        blocks.append(swap_blocks([in_ref[4 * quad + i, mine] for i in range(4)]))

    def value(index, c):
        top = (index * 2 + c) * PART
        rows = []
        for t in range(4):
            lanes = []
            for slot in range(SLOTS):
                at = top + slot * GROUPS
                for quad in range(ROWS // 4):
                    lanes.append(blocks[quad][t][at : at + GROUPS])
            rows.append(jnp.concatenate(lanes, axis=1))
        return jnp.concatenate(rows, axis=0)

    cosine = lanes_ref[0:1, :]
    sine = lanes_ref[1:2, :]

    def turned(index):
        re, im = value(index, 0), value(index, 1)
        return (re * cosine + im * sine, im * cosine - re * sine)

    v_base, v_slope, v_curve, g_base, g_slope = [turned(i) for i in range(5)]
    along, across = wave_ref[0], wave_ref[1]
    stream, span = wave_ref[2], wave_ref[3]

    def times_i(pair):
        return (-pair[1], pair[0])

    fields = [
        times_i([along * v_slope[c] - across * g_base[c] for c in range(2)]),
        v_base,
        times_i([across * v_slope[c] + along * g_base[c] for c in range(2)]),
        times_i(
            [across * v_curve[c] + along * g_slope[c] - span * v_base[c] for c in range(2)]
        ),
        g_base,
        times_i(
            [stream * v_base[c] - along * v_curve[c] + across * g_slope[c] for c in range(2)]
        ),
    ]
    for f, pair in enumerate(fields):
        top = (plane * 6 + f) * 2 * XL
        re_high, re_low = split(pair[0])
        im_high, im_low = split(pair[1])
        dh[top : top + XL, :] = re_high
        dl[top : top + XL, :] = re_low
        dh[top + XL : top + 2 * XL, :] = im_high
        dl[top + XL : top + 2 * XL, :] = im_low
        eh[top : top + XL, :] = -im_high
        el[top : top + XL, :] = -im_low
        eh[top + XL : top + 2 * XL, :] = re_high
        el[top + XL : top + 2 * XL, :] = re_low


def span_inverse(received, first, count, wave, lanes, tables):
    out = in_hbm((COLS, count, ZL, 12 * XL))
    args = [wave, lanes]
    rows = HALF_Z // SPAN_STEPS
    return pl.pallas_call(
        functools.partial(span_inverse_kernel, first, count),
        grid=(SPAN_STEPS,),
        in_specs=[on_chip()]
        + [fixed(a.shape) for a in args]
        + [fixed((rows, KZ))] * 4,
        out_specs=pl.BlockSpec((COLS // SPAN_STEPS, count, ZL, 12 * XL), lambda j: (j, 0, 0, 0)),
        out_shape=out,
        scratch_shapes=[pltpu.VMEM((count * 12 * XL, KZ), BF16)] * 4,
        compiler_params=params(32),
        name="span_inverse",
    )(received, *args, *tables)


BLOCK_X = 256


def product_kernel(count, in_ref, ch, cl, sh, sl, fch, fcl, fsh, fsl, out_ref, modes):
    for quad in range(COLS // 4):
        for column in range(3):
            tiles = [in_ref[4 * quad + i, 0, :, column * 128 : column * 128 + 128] for i in range(4)]
            for slot, tile in enumerate(swap_blocks(tiles)):
                top = (2 * column + slot // 2) * ZL
                modes[slot % 2, top : top + ZL, quad * 128 : quad * 128 + 128] = tile
    real = split(modes[0])
    imag = split(modes[1])
    total_re, total_im = None, None
    for block in range(HALF_X // BLOCK_X):
        here = slice(block * BLOCK_X, (block + 1) * BLOCK_X)
        even = triple(dot_nn, real, [ch[:, here], cl[:, here]])
        odd = triple(dot_nn, imag, [sh[:, here], sl[:, here]])

        def products(field):
            u, v, w, ox, oy, oz = [field[i * ZL : (i + 1) * ZL] for i in range(6)]
            return [v * oz - w * oy, w * ox - u * oz, u * oy - v * ox]

        right = products(even + odd)
        left = products(even - odd)

        def ordered(values):
            zeros = jnp.zeros((256 - 3 * ZL, BLOCK_X), F32)
            pieces = [x[:64] for x in values] + [x[64:] for x in values] + [zeros]
            return split(jnp.concatenate(pieces, axis=0))

        sums = ordered([r + l for r, l in zip(right, left)])
        gaps = ordered([r - l for r, l in zip(right, left)])
        part_re = triple(dot_nt, [fch[:, here], fcl[:, here]], sums)
        part_im = triple(dot_nt, [fsh[:, here], fsl[:, here]], gaps)
        total_re = part_re if total_re is None else total_re + part_re
        total_im = part_im if total_im is None else total_im + part_im
    lane = lax.broadcasted_iota(jnp.int32, (KX, 128), 1)
    last_re, last_im = total_re[:, 128:], total_im[:, 128:]
    third = jnp.where(lane < 64, last_re, pltpu.roll(last_im, 64, 1))
    ends = jnp.where(lane < 24, pltpu.roll(last_re, 64, 1), pltpu.roll(last_im, 88, 1))
    lane3 = lax.broadcasted_iota(jnp.int32, (COLS, XL, 128), 2)
    tail = slice(384 * count, 384 * count + 128)
    for plane in range(count):

        @pl.when(pl.program_id(0) == plane)
        def _():
            at = 384 * plane
            out_ref[:, :, at : at + 128] = total_re[:, :128].reshape(COLS, XL, 128)
            out_ref[:, :, at + 128 : at + 256] = total_im[:, :128].reshape(COLS, XL, 128)
            out_ref[:, :, at + 256 : at + 384] = third.reshape(COLS, XL, 128)
            if plane == 0:
                out_ref[:, :, tail] = jnp.where(lane3 < 48, ends.reshape(COLS, XL, 128), 0.0)
            else:
                moved = jnp.where(lane < 96, pltpu.roll(ends, 48, 1), 0.0).reshape(COLS, XL, 128)
                out_ref[:, :, tail] = jnp.where(lane3 < 48, out_ref[:, :, tail], moved)


def stream_products(received, tables):
    count = received.shape[1]
    out = in_hbm((COLS, XL, 384 * count + 128))
    return pl.pallas_call(
        functools.partial(product_kernel, count),
        grid=(count,),
        in_specs=[pl.BlockSpec((COLS, 1, ZL, 12 * XL), lambda p: (0, p, 0, 0))]
        + [fixed(a.shape) for a in tables],
        out_specs=whole(out.shape),
        out_shape=out,
        scratch_shapes=[pltpu.VMEM((2, 6 * ZL, KX), F32)],
        compiler_params=params(32),
        name="stream_products",
    )(received, *tables)


HOME_ROWS = 2 * 3 * PART


def span_forward_kernel(count, in_ref, lanes_ref, ch, cl, sh, sl, *rest):
    out_ref, left_high, left_low, right_high, right_low = rest[-5:]

    for plane in range(count):
        e_rows, o_rows = span_pairs(in_ref, plane, count)
        rows = slice(plane * 6 * XL, (plane + 1) * 6 * XL)
        left_high[rows], left_low[rows] = split(jnp.concatenate(e_rows, axis=0))
        right_high[rows], right_low[rows] = split(jnp.concatenate(o_rows, axis=0))

    result = triple(dot_nn, [left_high[...], left_low[...]], [ch[...], cl[...]]) + triple(
        dot_nn, [right_high[...], right_low[...]], [sh[...], sl[...]]
    )
    cosine = lanes_ref[0:1, :]
    sine = lanes_ref[1:2, :]
    for plane in range(count):
        top = plane * 6 * XL
        re, im = result[top : top + 3 * XL], result[top + 3 * XL : top + 6 * XL]
        turned = [re * cosine - im * sine, re * sine + im * cosine]
        for c in range(2):
            for h in range(3):
                block = turned[c][h * XL : (h + 1) * XL]
                row = plane * 6 * GROUPS + (c * 3 + h) * GROUPS
                for slot in range(SLOTS):
                    for quad in range(ROWS // 4):
                        at = slot * 256 + quad * 128
                        tiles = [block[t * 8 : t * 8 + 8, at : at + 128] for t in range(4)]
                        for i, tile in enumerate(swap_blocks(tiles)):
                            out_ref[4 * quad + i, slot, row : row + GROUPS, :] = tile


def span_pairs(in_ref, plane, count):
    lane = lax.broadcasted_iota(jnp.int32, (XL, 128), 1)
    low64 = lane < 64
    at = 384 * plane

    def pieces(index):
        offsets = [at, at + 128, at + 256, 384 * count]
        return [in_ref[index, :, o : o + 128] for o in offsets]

    sums, gaps = [], []
    for pair in range(8):
        plus, minus = pieces(2 * pair), pieces(2 * pair + 1)
        sums.append([p + m for p, m in zip(plus, minus)])
        gaps.append([p - m for p, m in zip(plus, minus)])

    def turn(value, amount):
        amount = amount % 128
        return pltpu.roll(value, amount, 1) if amount else value

    def ordered(values, c):
        main = [[], [], []]
        for i in range(0, 8, 2):
            a, b = values[i][c], values[i + 1][c]
            main[0].append(jnp.where(low64, a, turn(b, 64)))
            main[1].append(jnp.where(low64, turn(a, 64), b))
            a, b = values[i][2], values[i + 1][2]
            if c == 0:
                main[2].append(jnp.where(low64, a, turn(b, 64)))
            else:
                main[2].append(jnp.where(low64, turn(a, 64), b))
        tails = [None, None]
        for i in range(8):
            start = 24 * i
            moved = turn(values[i][3], start - 24 * (2 * plane + c))
            for half in range(2):
                low, high = max(start - 128 * half, 0), min(start + 24 - 128 * half, 128)
                if low >= high:
                    continue
                inside = (lane >= low) & (lane < high)
                rest = jnp.zeros_like(moved) if tails[half] is None else tails[half]
                tails[half] = jnp.where(inside, moved, rest)
        out = []
        for h in range(3):
            ends = []
            for half in range(2):
                index = lane + 128 * half
                mine = ((index // 8) % 3 == h) & (index < 192)
                ends.append(jnp.where(mine, tails[half], 0.0))
            out.append(jnp.concatenate(main[h] + ends, axis=1))
        return out

    even = ordered(sums, 0) + ordered(sums, 1)
    odd = ordered(gaps, 1) + [-x for x in ordered(gaps, 0)]
    return even, odd


def span_forward(received, first, count, lanes, tables, earlier):
    out = in_hbm((ROWS, SLOTS, CHUNKS * 6 * GROUPS, 128))
    before = [] if earlier is None else [earlier]
    return pl.pallas_call(
        functools.partial(span_forward_kernel, count),
        grid=(1,),
        in_specs=[on_chip(), fixed(lanes.shape)]
        + [fixed((KZ, KZ))] * 4
        + [pl.BlockSpec(memory_space=pl.ANY)] * len(before),
        out_specs=pl.BlockSpec(
            (ROWS, SLOTS, count * 6 * GROUPS, 128), lambda s: (0, 0, first // count, 0)
        ),
        out_shape=out,
        scratch_shapes=[pltpu.VMEM((count * 6 * XL, KZ), BF16)] * 4,
        input_output_aliases={2 + len(tables): 0} if before else {},
        compiler_params=params(20),
        name="span_forward",
    )(received, lanes, *tables, *before)


COMBINE_STEP = 2


def combine_kernel(in_ref, factor_ref, inverse_ref, vort_ref, lapv_ref):
    def stacked(value):
        high = value.astype(BF16).astype(F32)
        return high, value - high

    def right(index):
        high, low = stacked(inverse_ref[index])
        return jnp.concatenate([high, high, low], axis=0)

    first, second = right(0), right(1)
    both = jnp.concatenate([second, first], axis=0).astype(BF16)
    first = first.astype(BF16)
    for sub in range(COMBINE_STEP):
        group = pl.program_id(0) * COMBINE_STEP + sub
        g_lanes, s_lanes = [], []
        for slot in range(SLOTS):
            factors = [factor_ref[i, pl.ds(slot * GROUPS + group, 1), :] for i in range(5)]

            def field(h, c):
                row = slot * CHUNKS * 6 * GROUPS + (c * 3 + h) * GROUPS + group
                return jnp.concatenate(
                    [
                        in_ref[pl.ds(chunk * 6 * GROUPS + row, ROWS, stride=CHUNKS * HOME_ROWS), :]
                        for chunk in range(CHUNKS)
                    ],
                    axis=0,
                )

            hx = [field(0, c) for c in range(2)]
            hy = [field(1, c) for c in range(2)]
            hz = [field(2, c) for c in range(2)]
            for c in range(2):
                other = 1 - c
                g_term = factors[0] * hx[other] - factors[1] * hz[other]
                s_term = factors[2] * hx[other] + factors[3] * hz[other]
                if c == 0:
                    g_term = -g_term
                else:
                    s_term = -s_term
                y_term = factors[4] * hy[c]
                gh, gl = stacked(g_term)
                sh, sl = stacked(s_term)
                yh, yl = stacked(y_term)
                g_lanes.append(jnp.concatenate([gh, gl, gh], axis=0))
                s_lanes.append(jnp.concatenate([sh, sl, sh, yh, yl, yh], axis=0))
        g_left = jnp.concatenate(g_lanes, axis=1).astype(BF16)
        s_left = jnp.concatenate(s_lanes, axis=1).astype(BF16)
        vort = dot_tn(g_left, first)
        lapv = dot_tn(s_left, both)
        for slot in range(SLOTS):
            for c in range(2):
                for t in range(4):
                    row = (slot * 2 + c) * 128 + t * 32
                    vort_ref[c, 4 * sub + t, 32 * slot : 32 * slot + 32, :] = vort[row : row + 32]
                    lapv_ref[c, 4 * sub + t, 32 * slot : 32 * slot + 32, :] = lapv[row : row + 32]


def combine_planes(received, factors, inverse_ops):
    out = in_hbm((2, XL, KL, NY))
    args = [received, factors, jnp.swapaxes(inverse_ops, 1, 2)]
    block = pl.BlockSpec((2, 4 * COMBINE_STEP, KL, NY), lambda q: (0, q, 0, 0))
    return pl.pallas_call(
        combine_kernel,
        grid=(GROUPS // COMBINE_STEP,),
        in_specs=[on_chip()] + [fixed(a.shape) for a in args[1:]],
        out_specs=[block, block],
        out_shape=[out, out],
        compiler_params=params(24),
        name="combine_planes",
    )(*args)


def span_wave_arrays():
    row = jnp.arange(XL, dtype=jnp.int32)
    x = 4 * (row % GROUPS) + row // GROUPS + lax.axis_index("col") * XL
    stream = (STREAM_STEP * x.astype(F32))[:, None]
    signed = jnp.asarray(span_signed(span_order()), jnp.int32)
    span = (SPAN_STEP * signed.astype(F32))[None, :]
    square = stream * stream + span * span
    recip = 1.0 / jnp.where(square > 0, square, 1.0)
    full = jnp.zeros_like(square)
    return jnp.stack([stream * recip, span * recip, stream + full, span + full], axis=0)


def home_factors():
    part = jnp.arange(PART, dtype=jnp.int32)[:, None]
    lane = jnp.arange(128, dtype=jnp.int32)[None, :]
    x = 4 * (part % GROUPS) + lane // 32 + lax.axis_index("col") * XL
    k = 32 * (part // GROUPS) + lane % 32 + lax.axis_index("row") * KL
    stream = STREAM_STEP * x.astype(F32)
    span = SPAN_STEP * jnp.where(k < KZ // 2, k, k - KZ).astype(F32)
    square = stream * stream + span * span
    damp_g = 1.0 / jnp.sqrt(1.0 + square)
    damp_v = 1.0 / (1.0 + square)
    return jnp.stack(
        [damp_g * span, damp_g * stream, damp_v * stream, damp_v * span, -damp_v * square], axis=0
    )


def exchange(value, axis):
    return lax.all_to_all(value, axis, split_axis=0, concat_axis=0, tiled=True)


def per_device(v_coef, vort_coef, plane_ops, inverse_ops):
    def constants(arrays):
        return [kept_in_hbm(jnp.asarray(a)) for a in arrays]

    span_in = constants(span_inverse_tables())
    span_out = constants(span_forward_tables())
    stream = constants(stream_inverse_tables() + stream_forward_tables())
    lanes = jnp.asarray(span_lanes())
    wave = span_wave_arrays()
    factors = home_factors()
    values = plane_values(plane_ops, v_coef, vort_coef)
    pencils = exchange(values.reshape(ROWS, CHUNKS * PLANE_ROWS, 128), "row")
    spectral = None
    for first, count in SPANS:
        sent = span_inverse(pencils, first, count, wave, lanes, span_in)
        arrived = exchange(sent, "col")
        returned = exchange(stream_products(arrived, stream), "col")
        spectral = span_forward(returned, first, count, lanes, span_out, spectral)
    home = exchange(spectral.reshape(ROWS, CHUNKS * HOME_ROWS, 128), "row")
    home = home.reshape(ROWS * CHUNKS * HOME_ROWS, 128)
    vort_rhs, lapv_rhs = combine_planes(home, factors, inverse_ops)
    return (vort_rhs, lapv_rhs)


def solution(mesh):
    in_specs = (P(None, "col", "row", None), P(None, "col", "row", None), P(), P())
    out_specs = (P(None, "col", "row", None), P(None, "col", "row", None))
    return jax.shard_map(
        per_device, mesh=mesh, in_specs=in_specs, out_specs=out_specs, check_vma=False
    )
```

```python
import functools
import math

import jax
import jax.numpy as jnp
import ml_dtypes
import numpy as np
from jax import lax
from jax.experimental import pallas as pl
from jax.experimental.pallas import tpu as pltpu
from jax.sharding import PartitionSpec as P

STREAM_STEP = 0.25
SPAN_STEP = 2.0 / 3.0
ROWS = 8
COLS = 16
KX = 512
KZ = 768
NY = 256
PLANES = 24
CHUNKS = PLANES // ROWS
SPANS = ((2, 1), (0, 2))
XL = KX // COLS
KL = KZ // ROWS
POINTS_X = 3 * KX
POINTS_Z = 3 * KZ // 2
HALF_X = POINTS_X // 2
HALF_Z = POINTS_Z // 2
ZL = POINTS_Z // COLS
GROUPS = XL // 4
SLOTS = KL // 32
PART = SLOTS * GROUPS
F32 = jnp.float32
BF16 = jnp.bfloat16


def parts(table):
    table = np.asarray(table, np.float64)
    high = table.astype(np.float32).astype(ml_dtypes.bfloat16)
    low = (table - high.astype(np.float64)).astype(np.float32).astype(ml_dtypes.bfloat16)
    return [high, low]


def span_order():
    lane = np.arange(KZ)
    slot, rest = lane // (32 * ROWS), lane % (32 * ROWS)
    return (rest // 32) * KL + slot * 32 + rest % 32


def span_signed(modes):
    return np.where(modes < KZ // 2, modes, modes - KZ)


def stream_order():
    index = np.arange(KX)
    col, rest = index // XL, index % XL
    return col * XL + 4 * (rest % GROUPS) + rest // GROUPS


def span_angle(points):
    signed = span_signed(span_order())
    turn = np.mod((2 * points[:, None] + 1) * signed[None, :], 2 * POINTS_Z)
    return turn * (math.pi / POINTS_Z)


def span_inverse_tables():
    angle = span_angle(np.arange(HALF_Z))
    return parts(np.cos(angle)) + parts(np.sin(angle))


def span_forward_tables():
    main = (np.arange(8)[:, None] * ZL + np.arange(64)[None, :]).reshape(-1)
    tail = np.arange(8)[:, None, None] * ZL + 64 + np.arange(8)[None, None, :]
    tail = np.broadcast_to(tail, (8, 3, 8)).reshape(-1)
    points = np.concatenate([main, tail, np.zeros(64, np.int64)])
    used = (np.arange(points.size) < 704)[:, None]
    factor = used * (32.0 / POINTS_Z)
    angle = span_angle(points)
    return parts(np.cos(angle) * factor) + parts(np.sin(angle) * factor)


def stream_angle():
    turn = np.mod(stream_order()[:, None] * (2 * np.arange(HALF_X)[None, :] + 1), 2 * POINTS_X)
    return turn * (math.pi / POINTS_X)


def stream_inverse_tables():
    weight = np.where(stream_order() == 0, 1.0, 2.0)[:, None] / 32.0
    angle = stream_angle()
    return parts(weight * np.cos(angle)) + parts(-weight * np.sin(angle))


def stream_forward_tables():
    angle = stream_angle()
    return parts(np.cos(angle) / POINTS_X) + parts(-np.sin(angle) / POINTS_X)


def span_lanes():
    signed = span_signed(span_order())
    half = signed * (math.pi / POINTS_Z)
    rows = np.zeros((8, KZ), np.float32)
    rows[0] = np.cos(half)
    rows[1] = np.sin(half)
    return rows


def split(value):
    high = value.astype(BF16)
    low = (value - high.astype(F32)).astype(BF16)
    return high, low


def dot_nn(left, right):
    return lax.dot_general(left, right, (((1,), (0,)), ((), ())), preferred_element_type=F32)


def dot_nt(left, right):
    return lax.dot_general(left, right, (((1,), (1,)), ((), ())), preferred_element_type=F32)


def dot_tn(left, right):
    return lax.dot_general(left, right, (((0,), (0,)), ((), ())), preferred_element_type=F32)


def triple(dot, left, right):
    return dot(left[0], right[0]) + (dot(left[0], right[1]) + dot(left[1], right[0]))


def swap_blocks(tiles):
    lane = lax.broadcasted_iota(jnp.int32, tiles[0].shape, 1)
    low64 = lane < 64
    low32 = (lane & 32) == 0

    def turn(value, amount):
        return pltpu.roll(value, amount, 1)

    a0 = jnp.where(low64, tiles[0], turn(tiles[2], 64))
    a2 = jnp.where(low64, turn(tiles[0], 64), tiles[2])
    a1 = jnp.where(low64, tiles[1], turn(tiles[3], 64))
    a3 = jnp.where(low64, turn(tiles[1], 64), tiles[3])
    b0 = jnp.where(low32, a0, turn(a1, 32))
    b1 = jnp.where(low32, turn(a0, 96), a1)
    b2 = jnp.where(low32, a2, turn(a3, 32))
    b3 = jnp.where(low32, turn(a2, 96), a3)
    return [b0, b1, b2, b3]


def whole(shape):
    zeros = (0,) * len(shape)
    return pl.BlockSpec(shape, lambda *_: zeros)


def fixed(shape):
    zeros = (0,) * len(shape)
    return pl.BlockSpec(shape, lambda *_: zeros, pipeline_mode=pl.Buffered(1))


def on_chip():
    return pl.BlockSpec(memory_space=pltpu.VMEM)


def in_hbm(shape):
    return pltpu.HBM(shape, F32)


def kept_in_hbm(value):
    return pltpu.with_memory_space_constraint(value, pltpu.HBM)


def params(megabytes):
    return pltpu.CompilerParams(
        dimension_semantics=("arbitrary",), vmem_limit_bytes=megabytes * 1024 * 1024
    )


PLANE_ROWS = 5 * 2 * PART
PLANE_STEP = 4


def plane_kernel(ops_ref, v_ref, g_ref, out_ref):
    zero = jnp.zeros((128 - 3 * PLANES, NY), F32)
    high, low = split(jnp.concatenate([ops_ref[...], zero], axis=0))
    both = jnp.concatenate([high, low], axis=0)
    for sub in range(PLANE_STEP):
        group = pl.program_id(0) * PLANE_STEP + sub

        def values(ref):
            pieces = []
            for c in range(2):
                for slot in range(SLOTS):
                    for t in range(4):
                        pieces.append(ref[c, 4 * sub + t, 32 * slot : 32 * slot + 32, :])
            rows_high, rows_low = split(jnp.concatenate(pieces, axis=0))
            first = dot_nt(rows_high, both)
            return jnp.transpose(first[:, :128] + (first[:, 128:] + dot_nt(rows_low, high)))

        v_values = values(v_ref)
        g_values = values(g_ref)
        for value in range(5):
            source = v_values if value < 3 else g_values
            first = (value if value < 3 else value - 3) * PLANES
            for chunk in range(CHUNKS):
                top = first + chunk * ROWS
                for c in range(2):
                    for slot in range(SLOTS):
                        lane = (c * SLOTS + slot) * 128
                        row = chunk * PLANE_ROWS + (value * 2 + c) * PART + slot * GROUPS + group
                        out_ref[pl.ds(row, ROWS, stride=CHUNKS * PLANE_ROWS), :] = source[
                            top : top + ROWS, lane : lane + 128
                        ]


def plane_values(plane_ops, v_coef, vort_coef):
    out = in_hbm((ROWS * CHUNKS * PLANE_ROWS, 128))
    coef = pl.BlockSpec((2, 4 * PLANE_STEP, KL, NY), lambda q: (0, q, 0, 0))
    return pl.pallas_call(
        plane_kernel,
        grid=(GROUPS // PLANE_STEP,),
        in_specs=[whole((3 * PLANES, NY)), coef, coef],
        out_specs=whole(out.shape),
        out_shape=out,
        compiler_params=params(44),
        name="plane_values",
    )(kept_in_hbm(plane_ops.reshape(3 * PLANES, NY)), kept_in_hbm(v_coef), kept_in_hbm(vort_coef))


SPAN_STEPS = 1


def span_inverse_kernel(first, count, in_ref, wave_ref, lanes_ref, ch, cl, sh, sl, out_ref, *scratch):
    dh, dl, eh, el = scratch

    @pl.when(pl.program_id(0) == 0)
    def _():
        for plane in range(count):
            span_fields(first, plane, in_ref, wave_ref, lanes_ref, dh, dl, eh, el)

    even = triple(dot_nt, [ch[...], cl[...]], [dh[...], dl[...]])
    odd = triple(dot_nt, [sh[...], sl[...]], [eh[...], el[...]])
    for pair in range(COLS // 2 // SPAN_STEPS):
        part = slice(pair * ZL, (pair + 1) * ZL)
        for plane in range(count):
            lanes = slice(plane * 12 * XL, (plane + 1) * 12 * XL)
            out_ref[2 * pair, plane] = even[part, lanes] + odd[part, lanes]
            out_ref[2 * pair + 1, plane] = even[part, lanes] - odd[part, lanes]


def span_fields(first, plane, in_ref, wave_ref, lanes_ref, dh, dl, eh, el):
    mine = slice((first + plane) * PLANE_ROWS, (first + plane + 1) * PLANE_ROWS)
    blocks = []
    for quad in range(ROWS // 4):
        blocks.append(swap_blocks([in_ref[4 * quad + i, mine] for i in range(4)]))

    def value(index, c):
        top = (index * 2 + c) * PART
        rows = []
        for t in range(4):
            lanes = []
            for slot in range(SLOTS):
                at = top + slot * GROUPS
                for quad in range(ROWS // 4):
                    lanes.append(blocks[quad][t][at : at + GROUPS])
            rows.append(jnp.concatenate(lanes, axis=1))
        return jnp.concatenate(rows, axis=0)

    cosine = lanes_ref[0:1, :]
    sine = lanes_ref[1:2, :]

    def turned(index):
        re, im = value(index, 0), value(index, 1)
        return (re * cosine + im * sine, im * cosine - re * sine)

    v_base, v_slope, v_curve, g_base, g_slope = [turned(i) for i in range(5)]
    along, across = wave_ref[0], wave_ref[1]
    stream, span = wave_ref[2], wave_ref[3]

    def times_i(pair):
        return (-pair[1], pair[0])

    fields = [
        times_i([along * v_slope[c] - across * g_base[c] for c in range(2)]),
        v_base,
        times_i([across * v_slope[c] + along * g_base[c] for c in range(2)]),
        times_i(
            [across * v_curve[c] + along * g_slope[c] - span * v_base[c] for c in range(2)]
        ),
        g_base,
        times_i(
            [stream * v_base[c] - along * v_curve[c] + across * g_slope[c] for c in range(2)]
        ),
    ]
    for f, pair in enumerate(fields):
        top = (plane * 6 + f) * 2 * XL
        re_high, re_low = split(pair[0])
        im_high, im_low = split(pair[1])
        dh[top : top + XL, :] = re_high
        dl[top : top + XL, :] = re_low
        dh[top + XL : top + 2 * XL, :] = im_high
        dl[top + XL : top + 2 * XL, :] = im_low
        eh[top : top + XL, :] = -im_high
        el[top : top + XL, :] = -im_low
        eh[top + XL : top + 2 * XL, :] = re_high
        el[top + XL : top + 2 * XL, :] = re_low


def span_inverse(received, first, count, wave, lanes, tables):
    out = in_hbm((COLS, count, ZL, 12 * XL))
    args = [wave, lanes]
    rows = HALF_Z // SPAN_STEPS
    return pl.pallas_call(
        functools.partial(span_inverse_kernel, first, count),
        grid=(SPAN_STEPS,),
        in_specs=[on_chip()]
        + [fixed(a.shape) for a in args]
        + [fixed((rows, KZ))] * 4,
        out_specs=pl.BlockSpec((COLS // SPAN_STEPS, count, ZL, 12 * XL), lambda j: (j, 0, 0, 0)),
        out_shape=out,
        scratch_shapes=[pltpu.VMEM((count * 12 * XL, KZ), BF16)] * 4,
        compiler_params=params(32),
        name="span_inverse",
    )(received, *args, *tables)


BLOCK_X = 256


def product_kernel(count, in_ref, ch, cl, sh, sl, fch, fcl, fsh, fsl, out_ref, modes):
    for quad in range(COLS // 4):
        for column in range(3):
            tiles = [in_ref[4 * quad + i, 0, :, column * 128 : column * 128 + 128] for i in range(4)]
            for slot, tile in enumerate(swap_blocks(tiles)):
                top = (2 * column + slot // 2) * ZL
                modes[slot % 2, top : top + ZL, quad * 128 : quad * 128 + 128] = tile
    real = split(modes[0])
    imag = split(modes[1])
    total_re, total_im = None, None
    for block in range(HALF_X // BLOCK_X):
        here = slice(block * BLOCK_X, (block + 1) * BLOCK_X)
        even = triple(dot_nn, real, [ch[:, here], cl[:, here]])
        odd = triple(dot_nn, imag, [sh[:, here], sl[:, here]])

        def products(field):
            u, v, w, ox, oy, oz = [field[i * ZL : (i + 1) * ZL] for i in range(6)]
            return [v * oz - w * oy, w * ox - u * oz, u * oy - v * ox]

        right = products(even + odd)
        left = products(even - odd)

        def ordered(values):
            zeros = jnp.zeros((256 - 3 * ZL, BLOCK_X), F32)
            pieces = [x[:64] for x in values] + [x[64:] for x in values] + [zeros]
            return split(jnp.concatenate(pieces, axis=0))

        sums = ordered([r + l for r, l in zip(right, left)])
        gaps = ordered([r - l for r, l in zip(right, left)])
        part_re = triple(dot_nt, [fch[:, here], fcl[:, here]], sums)
        part_im = triple(dot_nt, [fsh[:, here], fsl[:, here]], gaps)
        total_re = part_re if total_re is None else total_re + part_re
        total_im = part_im if total_im is None else total_im + part_im
    lane = lax.broadcasted_iota(jnp.int32, (KX, 128), 1)
    last_re, last_im = total_re[:, 128:], total_im[:, 128:]
    third = jnp.where(lane < 64, last_re, pltpu.roll(last_im, 64, 1))
    ends = jnp.where(lane < 24, pltpu.roll(last_re, 64, 1), pltpu.roll(last_im, 88, 1))
    lane3 = lax.broadcasted_iota(jnp.int32, (COLS, XL, 128), 2)
    tail = slice(384 * count, 384 * count + 128)
    for plane in range(count):

        @pl.when(pl.program_id(0) == plane)
        def _():
            at = 384 * plane
            out_ref[:, :, at : at + 128] = total_re[:, :128].reshape(COLS, XL, 128)
            out_ref[:, :, at + 128 : at + 256] = total_im[:, :128].reshape(COLS, XL, 128)
            out_ref[:, :, at + 256 : at + 384] = third.reshape(COLS, XL, 128)
            if plane == 0:
                out_ref[:, :, tail] = jnp.where(lane3 < 48, ends.reshape(COLS, XL, 128), 0.0)
            else:
                moved = jnp.where(lane < 96, pltpu.roll(ends, 48, 1), 0.0).reshape(COLS, XL, 128)
                out_ref[:, :, tail] = jnp.where(lane3 < 48, out_ref[:, :, tail], moved)


def stream_products(received, tables):
    count = received.shape[1]
    out = in_hbm((COLS, XL, 384 * count + 128))
    return pl.pallas_call(
        functools.partial(product_kernel, count),
        grid=(count,),
        in_specs=[pl.BlockSpec((COLS, 1, ZL, 12 * XL), lambda p: (0, p, 0, 0))]
        + [fixed(a.shape) for a in tables],
        out_specs=whole(out.shape),
        out_shape=out,
        scratch_shapes=[pltpu.VMEM((2, 6 * ZL, KX), F32)],
        compiler_params=params(32),
        name="stream_products",
    )(received, *tables)


HOME_ROWS = 2 * 3 * PART


def span_forward_kernel(count, in_ref, lanes_ref, ch, cl, sh, sl, *rest):
    out_ref, left_high, left_low, right_high, right_low = rest[-5:]

    for plane in range(count):
        e_rows, o_rows = span_pairs(in_ref, plane, count)
        rows = slice(plane * 6 * XL, (plane + 1) * 6 * XL)
        left_high[rows], left_low[rows] = split(jnp.concatenate(e_rows, axis=0))
        right_high[rows], right_low[rows] = split(jnp.concatenate(o_rows, axis=0))

    result = triple(dot_nn, [left_high[...], left_low[...]], [ch[...], cl[...]]) + triple(
        dot_nn, [right_high[...], right_low[...]], [sh[...], sl[...]]
    )
    cosine = lanes_ref[0:1, :]
    sine = lanes_ref[1:2, :]
    for plane in range(count):
        top = plane * 6 * XL
        re, im = result[top : top + 3 * XL], result[top + 3 * XL : top + 6 * XL]
        turned = [re * cosine - im * sine, re * sine + im * cosine]
        for c in range(2):
            for h in range(3):
                block = turned[c][h * XL : (h + 1) * XL]
                row = plane * 6 * GROUPS + (c * 3 + h) * GROUPS
                for slot in range(SLOTS):
                    for quad in range(ROWS // 4):
                        at = slot * 256 + quad * 128
                        tiles = [block[t * 8 : t * 8 + 8, at : at + 128] for t in range(4)]
                        for i, tile in enumerate(swap_blocks(tiles)):
                            out_ref[4 * quad + i, slot, row : row + GROUPS, :] = tile


def span_pairs(in_ref, plane, count):
    lane = lax.broadcasted_iota(jnp.int32, (XL, 128), 1)
    low64 = lane < 64
    at = 384 * plane

    def pieces(index):
        offsets = [at, at + 128, at + 256, 384 * count]
        return [in_ref[index, :, o : o + 128] for o in offsets]

    sums, gaps = [], []
    for pair in range(8):
        plus, minus = pieces(2 * pair), pieces(2 * pair + 1)
        sums.append([p + m for p, m in zip(plus, minus)])
        gaps.append([p - m for p, m in zip(plus, minus)])

    def turn(value, amount):
        amount = amount % 128
        return pltpu.roll(value, amount, 1) if amount else value

    def ordered(values, c):
        main = [[], [], []]
        for i in range(0, 8, 2):
            a, b = values[i][c], values[i + 1][c]
            main[0].append(jnp.where(low64, a, turn(b, 64)))
            main[1].append(jnp.where(low64, turn(a, 64), b))
            a, b = values[i][2], values[i + 1][2]
            if c == 0:
                main[2].append(jnp.where(low64, a, turn(b, 64)))
            else:
                main[2].append(jnp.where(low64, turn(a, 64), b))
        tails = [None, None]
        for i in range(8):
            start = 24 * i
            moved = turn(values[i][3], start - 24 * (2 * plane + c))
            for half in range(2):
                low, high = max(start - 128 * half, 0), min(start + 24 - 128 * half, 128)
                if low >= high:
                    continue
                inside = (lane >= low) & (lane < high)
                rest = jnp.zeros_like(moved) if tails[half] is None else tails[half]
                tails[half] = jnp.where(inside, moved, rest)
        out = []
        for h in range(3):
            ends = []
            for half in range(2):
                index = lane + 128 * half
                mine = ((index // 8) % 3 == h) & (index < 192)
                ends.append(jnp.where(mine, tails[half], 0.0))
            out.append(jnp.concatenate(main[h] + ends, axis=1))
        return out

    even = ordered(sums, 0) + ordered(sums, 1)
    odd = ordered(gaps, 1) + [-x for x in ordered(gaps, 0)]
    return even, odd


def span_forward(received, first, count, lanes, tables, earlier):
    out = in_hbm((ROWS, SLOTS, CHUNKS * 6 * GROUPS, 128))
    before = [] if earlier is None else [earlier]
    return pl.pallas_call(
        functools.partial(span_forward_kernel, count),
        grid=(1,),
        in_specs=[on_chip(), fixed(lanes.shape)]
        + [fixed((KZ, KZ))] * 4
        + [pl.BlockSpec(memory_space=pl.ANY)] * len(before),
        out_specs=pl.BlockSpec(
            (ROWS, SLOTS, count * 6 * GROUPS, 128), lambda s: (0, 0, first // count, 0)
        ),
        out_shape=out,
        scratch_shapes=[pltpu.VMEM((count * 6 * XL, KZ), BF16)] * 4,
        input_output_aliases={2 + len(tables): 0} if before else {},
        compiler_params=params(20),
        name="span_forward",
    )(received, lanes, *tables, *before)


COMBINE_STEP = 4


def combine_kernel(in_ref, factor_ref, inverse_ref, vort_ref, lapv_ref):
    def stacked(value):
        high = value.astype(BF16).astype(F32)
        return high, value - high

    def right(index):
        high, low = stacked(inverse_ref[index])
        return jnp.concatenate([high, high, low], axis=0)

    first, second = right(0), right(1)
    both = jnp.concatenate([second, first], axis=0).astype(BF16)
    first = first.astype(BF16)
    for sub in range(COMBINE_STEP):
        group = pl.program_id(0) * COMBINE_STEP + sub
        g_lanes, s_lanes = [], []
        for slot in range(SLOTS):
            factors = [factor_ref[i, pl.ds(slot * GROUPS + group, 1), :] for i in range(5)]

            def field(h, c):
                row = slot * CHUNKS * 6 * GROUPS + (c * 3 + h) * GROUPS + group
                return jnp.concatenate(
                    [
                        in_ref[pl.ds(chunk * 6 * GROUPS + row, ROWS, stride=CHUNKS * HOME_ROWS), :]
                        for chunk in range(CHUNKS)
                    ],
                    axis=0,
                )

            hx = [field(0, c) for c in range(2)]
            hy = [field(1, c) for c in range(2)]
            hz = [field(2, c) for c in range(2)]
            for c in range(2):
                other = 1 - c
                g_term = factors[0] * hx[other] - factors[1] * hz[other]
                s_term = factors[2] * hx[other] + factors[3] * hz[other]
                if c == 0:
                    g_term = -g_term
                else:
                    s_term = -s_term
                y_term = factors[4] * hy[c]
                gh, gl = stacked(g_term)
                sh, sl = stacked(s_term)
                yh, yl = stacked(y_term)
                g_lanes.append(jnp.concatenate([gh, gl, gh], axis=0))
                s_lanes.append(jnp.concatenate([sh, sl, sh, yh, yl, yh], axis=0))
        g_left = jnp.concatenate(g_lanes, axis=1).astype(BF16)
        s_left = jnp.concatenate(s_lanes, axis=1).astype(BF16)
        vort = dot_tn(g_left, first)
        lapv = dot_tn(s_left, both)
        for slot in range(SLOTS):
            for c in range(2):
                for t in range(4):
                    row = (slot * 2 + c) * 128 + t * 32
                    vort_ref[c, 4 * sub + t, 32 * slot : 32 * slot + 32, :] = vort[row : row + 32]
                    lapv_ref[c, 4 * sub + t, 32 * slot : 32 * slot + 32, :] = lapv[row : row + 32]


def combine_planes(received, factors, inverse_ops):
    out = in_hbm((2, XL, KL, NY))
    args = [received, factors, jnp.swapaxes(inverse_ops, 1, 2)]
    block = pl.BlockSpec((2, 4 * COMBINE_STEP, KL, NY), lambda q: (0, q, 0, 0))
    return pl.pallas_call(
        combine_kernel,
        grid=(GROUPS // COMBINE_STEP,),
        in_specs=[on_chip()] + [fixed(a.shape) for a in args[1:]],
        out_specs=[block, block],
        out_shape=[out, out],
        compiler_params=params(40),
        name="combine_planes",
    )(*args)


def span_wave_arrays():
    row = jnp.arange(XL, dtype=jnp.int32)
    x = 4 * (row % GROUPS) + row // GROUPS + lax.axis_index("col") * XL
    stream = (STREAM_STEP * x.astype(F32))[:, None]
    signed = jnp.asarray(span_signed(span_order()), jnp.int32)
    span = (SPAN_STEP * signed.astype(F32))[None, :]
    square = stream * stream + span * span
    recip = 1.0 / jnp.where(square > 0, square, 1.0)
    full = jnp.zeros_like(square)
    return jnp.stack([stream * recip, span * recip, stream + full, span + full], axis=0)


def home_factors():
    part = jnp.arange(PART, dtype=jnp.int32)[:, None]
    lane = jnp.arange(128, dtype=jnp.int32)[None, :]
    x = 4 * (part % GROUPS) + lane // 32 + lax.axis_index("col") * XL
    k = 32 * (part // GROUPS) + lane % 32 + lax.axis_index("row") * KL
    stream = STREAM_STEP * x.astype(F32)
    span = SPAN_STEP * jnp.where(k < KZ // 2, k, k - KZ).astype(F32)
    square = stream * stream + span * span
    damp_g = 1.0 / jnp.sqrt(1.0 + square)
    damp_v = 1.0 / (1.0 + square)
    return jnp.stack(
        [damp_g * span, damp_g * stream, damp_v * stream, damp_v * span, -damp_v * square], axis=0
    )


def exchange(value, axis):
    return lax.all_to_all(value, axis, split_axis=0, concat_axis=0, tiled=True)


def per_device(v_coef, vort_coef, plane_ops, inverse_ops):
    def constants(arrays):
        return [kept_in_hbm(jnp.asarray(a)) for a in arrays]

    span_in = constants(span_inverse_tables())
    span_out = constants(span_forward_tables())
    stream = constants(stream_inverse_tables() + stream_forward_tables())
    lanes = jnp.asarray(span_lanes())
    wave = span_wave_arrays()
    factors = home_factors()
    values = plane_values(plane_ops, v_coef, vort_coef)
    pencils = exchange(values.reshape(ROWS, CHUNKS * PLANE_ROWS, 128), "row")
    spectral = None
    for first, count in SPANS:
        sent = span_inverse(pencils, first, count, wave, lanes, span_in)
        arrived = exchange(sent, "col")
        returned = exchange(stream_products(arrived, stream), "col")
        spectral = span_forward(returned, first, count, lanes, span_out, spectral)
    home = exchange(spectral.reshape(ROWS, CHUNKS * HOME_ROWS, 128), "row")
    home = home.reshape(ROWS * CHUNKS * HOME_ROWS, 128)
    vort_rhs, lapv_rhs = combine_planes(home, factors, inverse_ops)
    return (vort_rhs, lapv_rhs)


def solution(mesh):
    in_specs = (P(None, "col", "row", None), P(None, "col", "row", None), P(), P())
    out_specs = (P(None, "col", "row", None), P(None, "col", "row", None))
    return jax.shard_map(
        per_device, mesh=mesh, in_specs=in_specs, out_specs=out_specs, check_vma=False
    )
```
